256 devices in a mesh: row: 16 (over z, core), col: 8 (over x, y_lo), vec: 2 (over y_hi).
Axes of the slice: x: 4, y: 4 (y_hi: 2, y_lo: 2; y = y_hi * 2 + y_lo), z: 8, core: 2. Of those that a mesh axis runs over, the one named last changes fastest.
Arguments:
- vectors: bfloat16 [16, 131072], P('vec', ('row', 'col')), may hold values from -6 to 6
- tile_vals: bfloat16 [16, 8, 256, 128, 128], P('row', 'col'), may hold values from -0.09375 to 0.09375
- tile_rows: int32 [16, 8, 256], P('row', 'col'), may hold values from 0 to 1023, as said below
- tile_cols: int32 [16, 8, 256], P('row', 'col'), may hold values from 0 to 1023, as said below
- tile_counts: int32 [16, 8], P('row', 'col'), may hold values from 1 to 256, as said below
Outputs:
- product: bfloat16 [16, 131072], P('vec', ('row', 'col'))
- gram: float32 [16, 16], P(None, 'vec')
The draws below stay inside these ranges and needn't reach their ends.
Inputs may be any that keep to these rules, and one draw needn't show every extreme that they name: `tile_rows`: list [i, j] names tiles whose row index r has i * 64 <= r < (i + 1) * 64 and whose column index c has (c // 8) % (8) == j, that is the column's block of 8 tile rows, numbered c // 8, is held by column group j; live slots name distinct tiles with r >= c; slots at or beyond the count hold in-range indices that must be ignored. `tile_cols`: see tile_rows; the same slots. `tile_counts`: some lists are full in every draw; lists near the top of the triangle hold few tiles.
All inputs are finite; a program needn't handle non-finite values.
Results may differ from the reference program's by a relative error of at most 0.001.
Values may be sent and summed in bfloat16 or wider, within the bound.
A program may use at most 64 MiB of HBM per device.

```python
import math
import jax
import jax.numpy as jnp
from jax import lax

V = 16
TILE = 128
CH = 8
CAP = 256
NDIM = 131072
N_ROW = 16
N_COL = 8


def layout_lists(key):
    span = N_COL * CH
    full = span * N_ROW * CH
    place = jnp.arange(full, dtype=jnp.int32)
    inner = place // (N_ROW * CH)
    rest = place % (N_ROW * CH)
    group = rest // CH
    offset = rest % CH
    dev_i = jnp.arange(N_ROW, dtype=jnp.int32)[:, None, None]
    dev_j = jnp.arange(N_COL, dtype=jnp.int32)[None, :, None]
    rows = dev_i * span + inner[None, None, :] + 0 * dev_j
    cols = group[None, None, :] * span + dev_j * CH + offset[None, None, :] + 0 * dev_i
    valid = rows >= cols
    noise = jax.random.randint(jax.random.fold_in(key, 11), (N_ROW, N_COL, full), 0, 2 ** 17)
    score = jnp.where(valid, noise * full + place[None, None, :], -1)
    _, picked = lax.top_k(score, CAP)
    pick_rows = jnp.take_along_axis(rows, picked, axis=2).astype(jnp.int32)
    pick_cols = jnp.take_along_axis(cols, picked, axis=2).astype(jnp.int32)
    nvalid = jnp.sum(valid.astype(jnp.int32), axis=2)
    jitter = jax.random.randint(jax.random.fold_in(key, 12), (N_ROW, N_COL), 0, 4)
    counts = jnp.clip(nvalid * CAP * 3 // 2 // full - jitter, 1, CAP).astype(jnp.int32)
    return (pick_rows, pick_cols, counts)


def draw_tile_rows(key, part):
    return layout_lists(key)[0]


def draw_tile_cols(key, part):
    return layout_lists(key)[1]


def draw_tile_counts(key, part):
    return layout_lists(key)[2]


def level_of(rng, shape, split, low, high):
    loudness = 1.0
    for position, blocks in split:
        steps = jax.random.uniform(jax.random.fold_in(jax.random.fold_in(rng, 6), position), (blocks,), jnp.float32, low / len(split), high / len(split))
        loudness = loudness * jnp.repeat(jnp.exp(steps), shape[position] // blocks).reshape((-1,) + (1,) * (len(shape) - 1 - position))
    return loudness


def scatter_about(key, extent, spread, limit, shards=(), kind=jnp.bfloat16):
    drawn = spread * jax.random.normal(key, extent, jnp.float32)
    if shards:
        drawn = drawn * level_of(key, extent, shards, -0.22, 0.18)
    return jnp.clip(drawn, -limit, limit).astype(kind)


def setup_inputs(seed: int = 0) -> dict:
    splits = jax.random.split(jax.random.key(seed), 6)
    vectors = scatter_about(splits[0], (V, NDIM), 1.0, 6.0, ((0, 2), (1, 128)))
    tile_vals = scatter_about(splits[1], (N_ROW, N_COL, CAP, TILE, TILE), (TILE * CAP // CH) ** -0.5, 0.09375, ((0, 16), (1, 8)))
    tile_rows = draw_tile_rows(jax.random.fold_in(splits[5], 71), 0)
    tile_cols = draw_tile_cols(jax.random.fold_in(splits[5], 71), 0)
    tile_counts = draw_tile_counts(jax.random.fold_in(splits[5], 71), 0)
    return {"vectors": vectors, "tile_vals": tile_vals, "tile_rows": tile_rows, "tile_cols": tile_cols, "tile_counts": tile_counts}


def reference(vectors, tile_vals, tile_rows, tile_cols, tile_counts):
    vcount, ndim = vectors.shape
    tile = tile_vals.shape[-1]
    slots = tile_vals.shape[2]
    ntiles = ndim // tile
    blocks = vectors.astype(jnp.float32).reshape(vcount, ntiles, tile).transpose(1, 0, 2)
    flat_vals = tile_vals.reshape(-1, slots, tile, tile)
    flat_rows = tile_rows.reshape(-1, slots).astype(jnp.int32)
    flat_cols = tile_cols.reshape(-1, slots).astype(jnp.int32)
    flat_counts = tile_counts.reshape(-1).astype(jnp.int32)

    def step(total, item):
        vals, rows, cols, count = item
        live = jnp.arange(slots, dtype=jnp.int32) < count
        mirror = live & (rows != cols)
        vals32 = vals.astype(jnp.float32)
        down = jnp.einsum('tij,tvj->tvi', vals32, blocks[cols], precision=lax.Precision.HIGHEST)
        upper = jnp.einsum('tij,tvi->tvj', vals32, blocks[rows], precision=lax.Precision.HIGHEST)
        down = down * live.astype(jnp.float32)[:, None, None]
        upper = upper * mirror.astype(jnp.float32)[:, None, None]
        total = total.at[rows].add(down).at[cols].add(upper)
        return (total, None)
    start = jnp.zeros((ntiles, vcount, tile), jnp.float32)
    total, _ = lax.scan(step, start, (flat_vals, flat_rows, flat_cols, flat_counts))
    image = total.transpose(1, 0, 2).reshape(vcount, ndim)
    gram = jnp.dot(vectors.astype(jnp.float32), image.T, precision=lax.Precision.HIGHEST) / math.sqrt(ndim)
    return (image.astype(jnp.bfloat16), gram)
```

```python
import functools
import math

import jax
import jax.numpy as jnp
from jax import lax
from jax.experimental import pallas as pl
from jax.experimental.pallas import tpu as pltpu
from jax.sharding import PartitionSpec as P

MESH = pl.DeviceIdType.MESH
BF16 = jnp.bfloat16
F32 = jnp.float32
CHUNKS = 8


def split_hi_lo(value):
    hi = value.astype(BF16)
    lo = (value - hi.astype(F32)).astype(BF16)
    return hi, lo


def kernel(
    n_row, n_col, scale,
    rows_s, cols_s, count_s, rows_v, cols_v, x_ref, tiles_hbm,
    prod_ref, gram_ref,
    tiles, x_mine, x_row, x_oth, x_col, upper, down, col_part, exch, z_acc, z_recv, row_part, row_recv, acc,
    g1_send, g1_recv, g2_send, g2_recv,
    tile_sem, mine_sem, xz_s, xz_r, xf_s, xf_r, xr_s, xr_r, xo_s, xo_r, ex_s, ex_r, zs_s, zs_r, rs_s, rs_r,
    g1_s, g1_r, g2_s, g2_r,
):
    n_z = n_row // 2
    slots = tiles.shape[0]
    tile = tiles.shape[1]
    vloc = x_ref.shape[0]
    ch = x_ref.shape[1] // tile
    blk = ch * vloc
    span = n_col * ch
    per = slots // CHUNKS
    span_bits = span.bit_length() - 1
    row = lax.axis_index("row")
    col = lax.axis_index("col")
    vec = lax.axis_index("vec")
    z = row // 2
    core = row % 2
    oth = 1 - vec

    def tile_copy(c):
        part = pl.ds(c * per, per)
        return pltpu.make_async_copy(tiles_hbm.at[0, 0, part], tiles.at[part], tile_sem.at[c])

    def mine_copy(m):
        return pltpu.make_async_copy(x_ref.at[:, pl.ds(m * tile, tile)], x_mine.at[m], mine_sem.at[m])

    for m in range(ch):
        mine_copy(m).start()
    for c in range(CHUNKS):
        tile_copy(c).start()

    barrier = pltpu.get_barrier_semaphore()
    for d in range(1, n_row):
        pl.semaphore_signal(barrier, inc=1, device_id={"row": (row + d) % n_row}, device_id_type=MESH)
    for d in range(1, n_col):
        pl.semaphore_signal(barrier, inc=1, device_id={"col": (col + d) % n_col}, device_id_type=MESH)
    for d in range(n_col):
        pl.semaphore_signal(barrier, inc=1, device_id={"col": (col + d) % n_col, "vec": oth}, device_id_type=MESH)
    for m in range(ch):
        mine_copy(m).wait()
    pl.semaphore_wait(barrier, n_row - 1 + 2 * n_col - 1)

    def remote(src, dst, send, recv, to):
        return pltpu.make_async_remote_copy(
            src_ref=src, dst_ref=dst, send_sem=send, recv_sem=recv, device_id=to, device_id_type=MESH
        )

    far = sorted(range(1, n_z), key=lambda d: -min(d, n_z - d))

    def owned(k):
        return pl.ds(k * ch, ch)

    def x_up(d):
        return remote(x_mine, x_col.at[owned(row)], xz_s.at[d], xz_r.at[z], {"row": (row + 2 * d) % n_row})

    def x_side(d):
        return remote(x_mine, x_row.at[owned(col)], xr_s.at[d], xr_r.at[col], {"col": (col + d) % n_col})

    def x_over(d):
        return remote(
            x_mine, x_oth.at[owned(col)], xo_s.at[d], xo_r.at[col], {"col": (col + d) % n_col, "vec": oth}
        )

    for d in far:
        @pl.when(z + d < n_z)
        def _():
            x_up(d).start()
    for d in range(1, n_col):
        x_side(d).start()
    x_row[owned(col)] = x_mine[...]
    x_col[owned(row)] = x_mine[...]
    for k in range(2, n_row):
        @pl.when(k // 2 > z)
        def _():
            x_col[owned(k)] = jnp.zeros((ch, vloc, tile), BF16)
    count = count_s[0, 0]
    slot_iota = lax.broadcasted_iota(jnp.int32, (1, slots), 1)
    live = slot_iota < count
    rows_l = rows_v[0]
    cols_l = cols_v[0]

    mate = {"row": row + 1 - 2 * core}

    def x_mate():
        return remote(x_mine, x_col.at[owned(row)], xf_s.at[n_z], xf_r.at[n_z], mate)

    def x_forward(zz):
        part = x_col.at[owned(2 * zz + core)]
        return remote(part, part, xf_s.at[zz], xf_r.at[zz], mate)

    x_mate().start()

    def recv_wait(dst, sem):
        pltpu.make_async_copy(dst, dst, sem).wait()

    for d in range(1, n_col):
        src = (col + d) % n_col
        recv_wait(x_row.at[owned(src)], xr_r.at[src])
    for d in range(n_col):
        x_over(d).start()

    zero = jnp.zeros((2 * vloc, tile), BF16)

    def four(pick, first, out, trans):
        xs = [pick(first + q) for q in range(4)]
        a = [tiles[first + q] for q in range(4)]
        top = jnp.concatenate([xs[0], xs[1]], 0)
        bot = jnp.concatenate([xs[2], xs[3]], 0)
        left = jnp.concatenate([jnp.concatenate([top, zero], 0), jnp.concatenate([zero, bot], 0)], 1)
        if trans:
            w = jnp.concatenate([jnp.concatenate([a[0], a[1]], 0), jnp.concatenate([a[2], a[3]], 0)], 1)
            dims = (((1,), (1,)), ((), ()))
        else:
            w = jnp.concatenate([jnp.concatenate([a[0], a[1]], 1), jnp.concatenate([a[2], a[3]], 1)], 0)
            dims = (((1,), (0,)), ((), ()))
        r = lax.dot_general(left, w, dims, preferred_element_type=F32)
        base = pl.multiple_of(first * vloc, 4 * vloc)
        for q in range(4):
            side = q % 2
            out[pl.ds(base + q * vloc, vloc), :] = r[q * vloc:(q + 1) * vloc, side * tile:(side + 1) * tile]

    def pick_row(t):
        return x_row[rows_s[0, 0, t] & (span - 1)]

    def pick_col(t):
        c = cols_s[0, 0, t]
        return x_col[lax.shift_right_logical(c, span_bits) * ch + (c & (ch - 1))]

    def up_step(c, carry):
        tile_copy(c).wait()
        for q in range(per // 4):
            four(pick_row, c * per + 4 * q, upper, False)
        return carry

    lax.fori_loop(0, CHUNKS, up_step, 0)

    for d in far:
        @pl.when(z - d >= 0)
        def _():
            recv_wait(x_col.at[owned(2 * (z - d) + core)], xz_r.at[z - d])
            x_forward(z - d).start()

    def scatter(src, hot, dst):
        m = hot.shape[0]
        for p in range(vloc // 2):
            both = jnp.concatenate(
                [src[pl.ds(2 * p, slots, stride=vloc), :], src[pl.ds(2 * p + 1, slots, stride=vloc), :]], 1
            )
            hi, lo = split_hi_lo(both)
            res = jnp.dot(hot, hi, preferred_element_type=F32) + jnp.dot(hot, lo, preferred_element_type=F32)
            dst[pl.ds(2 * p, m, stride=vloc), :] = res[:, :tile]
            dst[pl.ds(2 * p + 1, m, stride=vloc), :] = res[:, tile:]

    def one_hot(place, m):
        hit = lax.broadcasted_iota(jnp.int32, (m, slots), 0) == place
        return jnp.where(hit, 1.0, 0.0).astype(BF16)

    group = cols_l // span
    col_place = (group % 2) * (n_z * ch) + (group // 2) * ch + cols_l % ch
    scatter(upper, one_hot(jnp.where(live & (rows_l != cols_l), col_place, -1), n_row * ch), col_part)

    half = n_z * blk
    swap = remote(
        col_part.at[pl.ds(pl.multiple_of((1 - core) * half, blk), half)], exch, ex_s, ex_r, mate
    )
    swap.start()

    recv_wait(x_col.at[owned(row + 1 - 2 * core)], xf_r.at[n_z])
    for d in far:
        @pl.when(z - d >= 0)
        def _():
            recv_wait(x_col.at[owned(2 * (z - d) + 1 - core)], xf_r.at[z - d])

    def down_step(c, carry):
        for q in range(per // 4):
            four(pick_col, c * per + 4 * q, down, True)
        return carry

    lax.fori_loop(0, CHUNKS // 2, down_step, 0)

    recv_wait(exch, ex_r)

    def z_block(zz):
        return pl.ds(pl.multiple_of(zz * blk, blk), blk)

    def z_send(d):
        return remote(
            z_acc.at[z_block(z - d)], z_recv.at[z], zs_s.at[d], zs_r.at[z], {"row": row - 2 * d}
        )

    mine = pl.multiple_of(core * half, blk)
    z_acc[...] = col_part[pl.ds(mine, half), :] + exch[...]
    for d in far:
        @pl.when(z - d >= 0)
        def _():
            z_send(d).start()

    lax.fori_loop(CHUNKS // 2, CHUNKS, down_step, 0)

    row_hot = jnp.concatenate(
        [
            one_hot(jnp.where(live, rows_l % span, -1), span),
            one_hot(jnp.where(live & (rows_l == cols_l), rows_l % ch, -1), 2 * ch),
        ],
        0,
    )
    scatter(down, row_hot, row_part)

    def r_send(d):
        to = (col + d) % n_col
        return remote(
            row_part.at[pl.ds(pl.multiple_of(to * blk, blk), blk)], row_recv.at[col], rs_s.at[d], rs_r.at[col],
            {"col": to},
        )

    for d in range(1, n_col):
        r_send(d).start()

    for d in range(n_col):
        recv_wait(x_oth.at[owned((col + d) % n_col)], xo_r.at[(col + d) % n_col])

    def against(base, j):
        part = jnp.concatenate(
            [row_part[pl.ds(base + m * vloc, vloc), :] for m in range(ch)], 1
        )
        hi, lo = split_hi_lo(part)
        left = jnp.concatenate([hi, lo], 0)
        right = jnp.concatenate(
            [
                jnp.concatenate([x[j * ch + m] for m in range(ch)], 1)
                for x in (x_row, x_oth)
            ],
            0,
        )
        r = lax.dot_general(left, right, (((1,), (1,)), ((), ())), preferred_element_type=F32)
        return r[:vloc] + r[vloc:]

    whole = against(0, 0)
    for jj in range(1, n_col):
        whole = whole + against(jj * blk, jj)
    off = whole - against(span * vloc, col)
    pad = jnp.zeros((vloc, tile - 4 * vloc), F32)
    g1_send[...] = jnp.concatenate([off, whole, pad], 1)

    def g1_side(d):
        return remote(g1_send, g1_recv.at[vec, col], g1_s.at[vec, d], g1_r.at[vec, col], {"col": (col + d) % n_col})

    def g1_over(d):
        return remote(
            g1_send, g1_recv.at[vec, col], g1_s.at[oth, d], g1_r.at[vec, col],
            {"col": (col + d) % n_col, "vec": oth},
        )

    for d in range(n_col):
        g1_over(d).start()
    for d in range(1, n_col):
        g1_side(d).start()

    image = row_part[pl.ds(pl.multiple_of(col * blk, blk), blk), :]
    for d in range(1, n_col):
        src = (col + d) % n_col
        recv_wait(row_recv.at[src], rs_r.at[src])
        image = image + row_recv[src]
    acc[...] = image + z_acc[z_block(z), :]

    own = g1_send[...]
    for d in range(1, n_col):
        src = (col + d) % n_col
        recv_wait(g1_recv.at[vec, src], g1_r.at[vec, src])
        own = own + g1_recv[vec, src]
    other = None
    for d in range(n_col):
        src = (col + d) % n_col
        recv_wait(g1_recv.at[oth, src], g1_r.at[oth, src])
        other = g1_recv[oth, src] if other is None else other + g1_recv[oth, src]
    lane = lax.broadcasted_iota(jnp.int32, (vloc, tile), 1)
    own = jnp.where(lane < 4 * vloc, own, pltpu.roll(other, 4 * vloc, 1))
    g2_send[...] = own

    def g2(d):
        return remote(g2_send, g2_recv.at[row], g2_s.at[d], g2_r.at[row], {"row": (row + d) % n_row})

    order = sorted(range(1, n_row), key=lambda d: -min(d, n_row - d))
    for d in order:
        g2(d).start()

    for d in range(n_z - 1, 0, -1):
        @pl.when(z + d < n_z)
        def _():
            src = (z + d) % n_z
            recv_wait(z_recv.at[src], zs_r.at[src])
            acc[...] += z_recv[src]

    for m in range(ch):
        prod_ref[:, m * tile:(m + 1) * tile] = acc[m * vloc:(m + 1) * vloc, :].astype(BF16)

    total = own
    for d in range(1, n_row):
        src = (row + d) % n_row
        recv_wait(g2_recv.at[src], g2_r.at[src])
        total = total + g2_recv[src]
    flip = jnp.transpose(total)
    g_own = total[:, :vloc] + flip[2 * vloc:3 * vloc, :]
    g_oth = pltpu.roll(total, tile - 5 * vloc, 1)[:, :vloc] + flip[3 * vloc:4 * vloc, :]
    gram_ref[pl.ds(pl.multiple_of(vec * vloc, vloc), vloc), :] = g_own * scale
    gram_ref[pl.ds(pl.multiple_of(oth * vloc, vloc), vloc), :] = g_oth * scale

    x_mate().wait_send()
    swap.wait_send()
    for d in range(1, n_z):
        @pl.when(z + d < n_z)
        def _():
            x_up(d).wait_send()

        @pl.when(z - d >= 0)
        def _():
            x_forward(z - d).wait_send()
            z_send(d).wait_send()
    for d in range(1, n_col):
        x_side(d).wait_send()
        r_send(d).wait_send()
        g1_side(d).wait_send()
    for d in range(n_col):
        x_over(d).wait_send()
        g1_over(d).wait_send()
    for d in range(1, n_row):
        g2(d).wait_send()


def shards(n_row, n_col, vectors, tile_vals, tile_rows, tile_cols, tile_counts):
    vloc, width = vectors.shape
    slots, tile = tile_vals.shape[2], tile_vals.shape[3]
    ch = width // tile
    blk = ch * vloc
    n_z = n_row // 2
    dma = pltpu.SemaphoreType.DMA
    vmem = functools.partial(pl.BlockSpec, memory_space=pltpu.VMEM)
    smem = functools.partial(pl.BlockSpec, memory_space=pltpu.SMEM)
    scale = 1.0 / math.sqrt(width * n_row * n_col)
    return pl.pallas_call(
        functools.partial(kernel, n_row, n_col, scale),
        out_shape=(
            jax.ShapeDtypeStruct((vloc, width), BF16),
            jax.ShapeDtypeStruct((2 * vloc, vloc), F32),
        ),
        in_specs=[smem(), smem(), smem(), vmem(), vmem(), vmem(), pl.BlockSpec(memory_space=pl.ANY)],
        out_specs=(vmem(), vmem()),
        scratch_shapes=[
            pltpu.VMEM((slots, tile, tile), BF16),
            pltpu.VMEM((ch, vloc, tile), BF16),
            pltpu.VMEM((n_col * ch, vloc, tile), BF16),
            pltpu.VMEM((n_col * ch, vloc, tile), BF16),
            pltpu.VMEM((n_row * ch, vloc, tile), BF16),
            pltpu.VMEM((slots * vloc, tile), F32),
            pltpu.VMEM((slots * vloc, tile), F32),
            pltpu.VMEM((n_row * blk, tile), F32),
            pltpu.VMEM((n_z * blk, tile), F32),
            pltpu.VMEM((n_z * blk, tile), F32),
            pltpu.VMEM((n_z, blk, tile), F32),
            pltpu.VMEM(((n_col + 2) * blk, tile), F32),
            pltpu.VMEM((n_col, blk, tile), F32),
            pltpu.VMEM((blk, tile), F32),
            pltpu.VMEM((vloc, tile), F32),
            pltpu.VMEM((2, n_col, vloc, tile), F32),
            pltpu.VMEM((vloc, tile), F32),
            pltpu.VMEM((n_row, vloc, tile), F32),
            dma((CHUNKS,)), dma((ch,)),
            dma((n_z,)), dma((n_z,)),
            dma((n_z + 1,)), dma((n_z + 1,)),
            dma((n_col,)), dma((n_col,)),
            dma((n_col,)), dma((n_col,)),
            dma(()), dma(()),
            dma((n_z,)), dma((n_z,)),
            dma((n_col,)), dma((n_col,)),
            dma((2, n_col)), dma((2, n_col)),
            dma((n_row,)), dma((n_row,)),
        ],
        compiler_params=pltpu.CompilerParams(
            collective_id=0, has_side_effects=True, vmem_limit_bytes=60 * 1024 * 1024
        ),
    )(tile_rows, tile_cols, tile_counts, tile_rows, tile_cols, vectors, tile_vals)


def solution(mesh):
    return jax.shard_map(
        functools.partial(shards, mesh.shape["row"], mesh.shape["col"]),
        mesh=mesh,
        in_specs=(
            P("vec", ("row", "col")),
            P("row", "col", None, None, None),
            P("row", "col", None),
            P("row", "col", None),
            P("row", "col"),
        ),
        out_specs=(P("vec", ("row", "col")), P(None, "vec")),
        check_vma=False,
    )
```

```python
import functools
import math

import jax
import jax.numpy as jnp
from jax import lax
from jax.experimental import pallas as pl
from jax.experimental.pallas import tpu as pltpu
from jax.sharding import PartitionSpec as P

MESH = pl.DeviceIdType.MESH
BF16 = jnp.bfloat16
F32 = jnp.float32
CHUNKS = 8


def split_hi_lo(value):
    hi = value.astype(BF16)
    lo = (value - hi.astype(F32)).astype(BF16)
    return hi, lo


def kernel(
    n_row, n_col, scale,
    rows_hbm, cols_hbm, count_hbm, x_ref, tiles_hbm,
    prod_ref, gram_ref,
    rows_s, cols_s, count_s, rows_v, cols_v, tiles, x_mine, x_row, x_oth, x_col, upper, down, col_part, exch, z_acc, z_recv, row_part, row_recv, acc,
    g1_send, g1_recv, g2_send, g2_recv,
    list_sem, tile_sem, mine_sem, xz_s, xz_r, xf_s, xf_r, xr_s, xr_r, xo_s, xo_r, ex_s, ex_r, zs_s, zs_r, rs_s, rs_r,
    g1_s, g1_r, g2_s, g2_r,
):
    n_z = n_row // 2
    slots = tiles.shape[0]
    tile = tiles.shape[1]
    vloc = x_ref.shape[0]
    ch = x_ref.shape[1] // tile
    blk = ch * vloc
    span = n_col * ch
    per = slots // CHUNKS
    span_bits = span.bit_length() - 1
    row = lax.axis_index("row")
    col = lax.axis_index("col")
    vec = lax.axis_index("vec")
    z = row // 2
    core = row % 2
    oth = 1 - vec

    def tile_copy(c):
        part = pl.ds(c * per, per)
        return pltpu.make_async_copy(tiles_hbm.at[0, 0, part], tiles.at[part], tile_sem.at[c])

    def mine_copy(m):
        return pltpu.make_async_copy(x_ref.at[:, pl.ds(m * tile, tile)], x_mine.at[m], mine_sem.at[m])

    lists = [
        pltpu.make_async_copy(src, dst, list_sem.at[q])
        for q, (src, dst) in enumerate(
            [(rows_hbm, rows_s), (cols_hbm, cols_s), (count_hbm, count_s), (rows_hbm, rows_v), (cols_hbm, cols_v)]
        )
    ]

    for m in range(ch):
        mine_copy(m).start()
    for q in lists:
        q.start()
    for c in range(CHUNKS):
        tile_copy(c).start()

    barrier = pltpu.get_barrier_semaphore()
    for d in range(1, n_row):
        pl.semaphore_signal(barrier, inc=1, device_id={"row": (row + d) % n_row}, device_id_type=MESH)
    for d in range(1, n_col):
        pl.semaphore_signal(barrier, inc=1, device_id={"col": (col + d) % n_col}, device_id_type=MESH)
    for d in range(n_col):
        pl.semaphore_signal(barrier, inc=1, device_id={"col": (col + d) % n_col, "vec": oth}, device_id_type=MESH)
    for m in range(ch):
        mine_copy(m).wait()
    pl.semaphore_wait(barrier, n_row - 1 + 2 * n_col - 1)

    def remote(src, dst, send, recv, to):
        return pltpu.make_async_remote_copy(
            src_ref=src, dst_ref=dst, send_sem=send, recv_sem=recv, device_id=to, device_id_type=MESH
        )

    far = sorted(range(1, n_z), key=lambda d: -min(d, n_z - d))

    def owned(k):
        return pl.ds(k * ch, ch)

    def x_up(d):
        return remote(x_mine, x_col.at[owned(row)], xz_s.at[d], xz_r.at[z], {"row": (row + 2 * d) % n_row})

    def x_side(d):
        return remote(x_mine, x_row.at[owned(col)], xr_s.at[d], xr_r.at[col], {"col": (col + d) % n_col})

    def x_over(d):
        return remote(
            x_mine, x_oth.at[owned(col)], xo_s.at[d], xo_r.at[col], {"col": (col + d) % n_col, "vec": oth}
        )

    for d in far:
        @pl.when(z + d < n_z)
        def _():
            x_up(d).start()
    for d in range(1, n_col):
        x_side(d).start()
    x_row[owned(col)] = x_mine[...]
    x_col[owned(row)] = x_mine[...]
    for k in range(2, n_row):
        @pl.when(k // 2 > z)
        def _():
            x_col[owned(k)] = jnp.zeros((ch, vloc, tile), BF16)
    for q in lists:
        q.wait()
    count = count_s[0, 0]
    slot_iota = lax.broadcasted_iota(jnp.int32, (1, slots), 1)
    live = slot_iota < count
    rows_l = rows_v[0]
    cols_l = cols_v[0]

    mate = {"row": row + 1 - 2 * core}

    def x_mate():
        return remote(x_mine, x_col.at[owned(row)], xf_s.at[n_z], xf_r.at[n_z], mate)

    def x_forward(zz):
        part = x_col.at[owned(2 * zz + core)]
        return remote(part, part, xf_s.at[zz], xf_r.at[zz], mate)

    x_mate().start()

    def recv_wait(dst, sem):
        pltpu.make_async_copy(dst, dst, sem).wait()

    for d in range(1, n_col):
        src = (col + d) % n_col
        recv_wait(x_row.at[owned(src)], xr_r.at[src])
    for d in range(n_col):
        x_over(d).start()

    zero = jnp.zeros((2 * vloc, tile), BF16)

    def four(pick, first, out, trans):
        xs = [pick(first + q) for q in range(4)]
        a = [tiles[first + q] for q in range(4)]
        top = jnp.concatenate([xs[0], xs[1]], 0)
        bot = jnp.concatenate([xs[2], xs[3]], 0)
        left = jnp.concatenate([jnp.concatenate([top, zero], 0), jnp.concatenate([zero, bot], 0)], 1)
        if trans:
            w = jnp.concatenate([jnp.concatenate([a[0], a[1]], 0), jnp.concatenate([a[2], a[3]], 0)], 1)
            dims = (((1,), (1,)), ((), ()))
        else:
            w = jnp.concatenate([jnp.concatenate([a[0], a[1]], 1), jnp.concatenate([a[2], a[3]], 1)], 0)
            dims = (((1,), (0,)), ((), ()))
        r = lax.dot_general(left, w, dims, preferred_element_type=F32)
        base = pl.multiple_of(first * vloc, 4 * vloc)
        for q in range(4):
            side = q % 2
            out[pl.ds(base + q * vloc, vloc), :] = r[q * vloc:(q + 1) * vloc, side * tile:(side + 1) * tile]

    def pick_row(t):
        return x_row[rows_s[0, 0, t] & (span - 1)]

    def pick_col(t):
        c = cols_s[0, 0, t]
        return x_col[lax.shift_right_logical(c, span_bits) * ch + (c & (ch - 1))]

    def up_step(c, carry):
        tile_copy(c).wait()
        for q in range(per // 4):
            four(pick_row, c * per + 4 * q, upper, False)
        return carry

    lax.fori_loop(0, CHUNKS, up_step, 0)

    for d in far:
        @pl.when(z - d >= 0)
        def _():
            recv_wait(x_col.at[owned(2 * (z - d) + core)], xz_r.at[z - d])
            x_forward(z - d).start()

    def scatter(src, hot, dst):
        m = hot.shape[0]
        for p in range(vloc // 2):
            both = jnp.concatenate(
                [src[pl.ds(2 * p, slots, stride=vloc), :], src[pl.ds(2 * p + 1, slots, stride=vloc), :]], 1
            )
            hi, lo = split_hi_lo(both)
            res = jnp.dot(hot, hi, preferred_element_type=F32) + jnp.dot(hot, lo, preferred_element_type=F32)
            dst[pl.ds(2 * p, m, stride=vloc), :] = res[:, :tile]
            dst[pl.ds(2 * p + 1, m, stride=vloc), :] = res[:, tile:]

    def one_hot(place, m):
        hit = lax.broadcasted_iota(jnp.int32, (m, slots), 0) == place
        return jnp.where(hit, 1.0, 0.0).astype(BF16)

    group = cols_l // span
    col_place = (group % 2) * (n_z * ch) + (group // 2) * ch + cols_l % ch
    scatter(upper, one_hot(jnp.where(live & (rows_l != cols_l), col_place, -1), n_row * ch), col_part)

    half = n_z * blk
    swap = remote(
        col_part.at[pl.ds(pl.multiple_of((1 - core) * half, blk), half)], exch, ex_s, ex_r, mate
    )
    swap.start()

    recv_wait(x_col.at[owned(row + 1 - 2 * core)], xf_r.at[n_z])
    for d in far:
        @pl.when(z - d >= 0)
        def _():
            recv_wait(x_col.at[owned(2 * (z - d) + 1 - core)], xf_r.at[z - d])

    def down_step(c, carry):
        for q in range(per // 4):
            four(pick_col, c * per + 4 * q, down, True)
        return carry

    lax.fori_loop(0, CHUNKS // 2, down_step, 0)

    recv_wait(exch, ex_r)

    def z_block(zz):
        return pl.ds(pl.multiple_of(zz * blk, blk), blk)

    def z_send(d):
        return remote(
            z_acc.at[z_block(z - d)], z_recv.at[z], zs_s.at[d], zs_r.at[z], {"row": row - 2 * d}
        )

    mine = pl.multiple_of(core * half, blk)
    z_acc[...] = col_part[pl.ds(mine, half), :] + exch[...]
    for d in far:
        @pl.when(z - d >= 0)
        def _():
            z_send(d).start()

    lax.fori_loop(CHUNKS // 2, CHUNKS, down_step, 0)

    row_hot = jnp.concatenate(
        [
            one_hot(jnp.where(live, rows_l % span, -1), span),
            one_hot(jnp.where(live & (rows_l == cols_l), rows_l % ch, -1), 2 * ch),
        ],
        0,
    )
    scatter(down, row_hot, row_part)

    def r_send(d):
        to = (col + d) % n_col
        return remote(
            row_part.at[pl.ds(pl.multiple_of(to * blk, blk), blk)], row_recv.at[col], rs_s.at[d], rs_r.at[col],
            {"col": to},
        )

    for d in range(n_col):
        recv_wait(x_oth.at[owned((col + d) % n_col)], xo_r.at[(col + d) % n_col])

    def against(base, j):
        part = jnp.concatenate(
            [row_part[pl.ds(base + m * vloc, vloc), :] for m in range(ch)], 1
        )
        hi, lo = split_hi_lo(part)
        left = jnp.concatenate([hi, lo], 0)
        right = jnp.concatenate(
            [
                jnp.concatenate([x[j * ch + m] for m in range(ch)], 1)
                for x in (x_row, x_oth)
            ],
            0,
        )
        r = lax.dot_general(left, right, (((1,), (1,)), ((), ())), preferred_element_type=F32)
        return r[:vloc] + r[vloc:]

    whole = against(0, 0)
    for jj in range(1, n_col):
        whole = whole + against(jj * blk, jj)
    off = whole - against(span * vloc, col)
    pad = jnp.zeros((vloc, tile - 4 * vloc), F32)
    g1_send[...] = jnp.concatenate([off, whole, pad], 1)

    def g1_side(d):
        return remote(g1_send, g1_recv.at[vec, col], g1_s.at[vec, d], g1_r.at[vec, col], {"col": (col + d) % n_col})

    def g1_over(d):
        return remote(
            g1_send, g1_recv.at[vec, col], g1_s.at[oth, d], g1_r.at[vec, col],
            {"col": (col + d) % n_col, "vec": oth},
        )

    for d in range(n_col):
        g1_over(d).start()
    for d in range(1, n_col):
        g1_side(d).start()
    for d in range(1, n_col):
        r_send(d).start()

    own = g1_send[...]
    for d in range(1, n_col):
        src = (col + d) % n_col
        recv_wait(g1_recv.at[vec, src], g1_r.at[vec, src])
        own = own + g1_recv[vec, src]
    other = None
    for d in range(n_col):
        src = (col + d) % n_col
        recv_wait(g1_recv.at[oth, src], g1_r.at[oth, src])
        other = g1_recv[oth, src] if other is None else other + g1_recv[oth, src]
    lane = lax.broadcasted_iota(jnp.int32, (vloc, tile), 1)
    own = jnp.where(lane < 4 * vloc, own, pltpu.roll(other, 4 * vloc, 1))
    g2_send[...] = own

    def g2(d):
        return remote(g2_send, g2_recv.at[row], g2_s.at[d], g2_r.at[row], {"row": (row + d) % n_row})

    order = sorted(range(1, n_row), key=lambda d: -min(d, n_row - d))
    for d in order:
        g2(d).start()

    image = row_part[pl.ds(pl.multiple_of(col * blk, blk), blk), :]
    for d in range(1, n_col):
        src = (col + d) % n_col
        recv_wait(row_recv.at[src], rs_r.at[src])
        image = image + row_recv[src]
    acc[...] = image + z_acc[z_block(z), :]

    for d in range(n_z - 1, 0, -1):
        @pl.when(z + d < n_z)
        def _():
            src = (z + d) % n_z
            recv_wait(z_recv.at[src], zs_r.at[src])
            acc[...] += z_recv[src]

    for m in range(ch):
        prod_ref[:, m * tile:(m + 1) * tile] = acc[m * vloc:(m + 1) * vloc, :].astype(BF16)

    total = own
    for d in range(1, n_row):
        src = (row + d) % n_row
        recv_wait(g2_recv.at[src], g2_r.at[src])
        total = total + g2_recv[src]
    flip = jnp.transpose(total)
    g_own = total[:, 2 * vloc:3 * vloc] + flip[:vloc, :vloc]
    g_oth = total[:, 3 * vloc:4 * vloc] + flip[5 * vloc:6 * vloc, :vloc]
    first = jnp.where(vec == 0, g_own, g_oth)
    second = jnp.where(vec == 0, g_oth, g_own)
    gram_ref[...] = jnp.concatenate([first, second], 1) * scale

    x_mate().wait_send()
    swap.wait_send()
    for d in range(1, n_z):
        @pl.when(z + d < n_z)
        def _():
            x_up(d).wait_send()

        @pl.when(z - d >= 0)
        def _():
            x_forward(z - d).wait_send()
            z_send(d).wait_send()
    for d in range(1, n_col):
        x_side(d).wait_send()
        r_send(d).wait_send()
        g1_side(d).wait_send()
    for d in range(n_col):
        x_over(d).wait_send()
        g1_over(d).wait_send()
    for d in range(1, n_row):
        g2(d).wait_send()


def shards(n_row, n_col, vectors, tile_vals, tile_rows, tile_cols, tile_counts):
    vloc, width = vectors.shape
    slots, tile = tile_vals.shape[2], tile_vals.shape[3]
    ch = width // tile
    blk = ch * vloc
    n_z = n_row // 2
    dma = pltpu.SemaphoreType.DMA
    vmem = functools.partial(pl.BlockSpec, memory_space=pltpu.VMEM)
    scale = 1.0 / math.sqrt(width * n_row * n_col)
    product, gram = pl.pallas_call(
        functools.partial(kernel, n_row, n_col, scale),
        out_shape=(
            pltpu.VMEM((vloc, width), BF16),
            pltpu.VMEM((vloc, 2 * vloc), F32),
        ),
        in_specs=[pl.BlockSpec(memory_space=pltpu.HBM)] * 5,
        out_specs=(vmem(), vmem()),
        scratch_shapes=[
            pltpu.SMEM((1, 1, slots), jnp.int32),
            pltpu.SMEM((1, 1, slots), jnp.int32),
            pltpu.SMEM((1, 1), jnp.int32),
            pltpu.VMEM((1, 1, slots), jnp.int32),
            pltpu.VMEM((1, 1, slots), jnp.int32),
            pltpu.VMEM((slots, tile, tile), BF16),
            pltpu.VMEM((ch, vloc, tile), BF16),
            pltpu.VMEM((n_col * ch, vloc, tile), BF16),
            pltpu.VMEM((n_col * ch, vloc, tile), BF16),
            pltpu.VMEM((n_row * ch, vloc, tile), BF16),
            pltpu.VMEM((slots * vloc, tile), F32),
            pltpu.VMEM((slots * vloc, tile), F32),
            pltpu.VMEM((n_row * blk, tile), F32),
            pltpu.VMEM((n_z * blk, tile), F32),
            pltpu.VMEM((n_z * blk, tile), F32),
            pltpu.VMEM((n_z, blk, tile), F32),
            pltpu.VMEM(((n_col + 2) * blk, tile), F32),
            pltpu.VMEM((n_col, blk, tile), F32),
            pltpu.VMEM((blk, tile), F32),
            pltpu.VMEM((vloc, tile), F32),
            pltpu.VMEM((2, n_col, vloc, tile), F32),
            pltpu.VMEM((vloc, tile), F32),
            pltpu.VMEM((n_row, vloc, tile), F32),
            dma((5,)), dma((CHUNKS,)), dma((ch,)),
            dma((n_z,)), dma((n_z,)),
            dma((n_z + 1,)), dma((n_z + 1,)),
            dma((n_col,)), dma((n_col,)),
            dma((n_col,)), dma((n_col,)),
            dma(()), dma(()),
            dma((n_z,)), dma((n_z,)),
            dma((n_col,)), dma((n_col,)),
            dma((2, n_col)), dma((2, n_col)),
            dma((n_row,)), dma((n_row,)),
        ],
        compiler_params=pltpu.CompilerParams(
            collective_id=0, has_side_effects=True, vmem_limit_bytes=60 * 1024 * 1024
        ),
    )(tile_rows, tile_cols, tile_counts, vectors, tile_vals)
    return product, gram.T


def solution(mesh):
    return jax.shard_map(
        functools.partial(shards, mesh.shape["row"], mesh.shape["col"]),
        mesh=mesh,
        in_specs=(
            P("vec", ("row", "col")),
            P("row", "col", None, None, None),
            P("row", "col", None),
            P("row", "col", None),
            P("row", "col"),
        ),
        out_specs=(P("vec", ("row", "col")), P(None, "vec")),
        check_vma=False,
    )
```

```python
import functools
import math

import jax
import jax.numpy as jnp
from jax import lax
from jax.experimental import pallas as pl
from jax.experimental.pallas import tpu as pltpu
from jax.sharding import PartitionSpec as P

MESH = pl.DeviceIdType.MESH
BF16 = jnp.bfloat16
F32 = jnp.float32
CHUNKS = 8


def split_hi_lo(value):
    hi = value.astype(BF16)
    lo = (value - hi.astype(F32)).astype(BF16)
    return hi, lo


def kernel(
    n_row, n_col, scale,
    count_v, rows_hbm, cols_hbm, x_ref, tiles_hbm,
    prod_ref, gram_ref,
    rows_s, cols_s, rows_v, cols_v, tiles, x_mine, x_row, x_oth, x_col, upper, down, col_part, exch, z_acc, z_recv, row_part, row_recv, acc,
    g1_send, g1_recv, g2_send, g2_recv,
    list_sem, mine_sem, tile_sem, x_s, xz_r, xf_r, xr_r, xo_r, z_s, ex_r, zs_r, o_s, rs_r, g1_r, g2_r,
):
    n_z = n_row // 2
    slots = tiles.shape[0]
    tile = tiles.shape[1]
    vloc = x_ref.shape[0]
    ch = x_ref.shape[1] // tile
    blk = ch * vloc
    span = n_col * ch
    per = slots // CHUNKS
    fold = vloc // 2
    span_bits = span.bit_length() - 1
    row = lax.axis_index("row")
    col = lax.axis_index("col")
    vec = lax.axis_index("vec")
    z = row // 2
    core = row % 2
    oth = 1 - vec

    def tile_copy(c):
        part = pl.ds(c * per, per)
        return pltpu.make_async_copy(tiles_hbm.at[0, 0, part], tiles.at[part], tile_sem)

    def mine_copy(m):
        return pltpu.make_async_copy(x_ref.at[:, pl.ds(m * tile, tile)], x_mine.at[m], mine_sem)

    lists = [
        pltpu.make_async_copy(rows_hbm, rows_s, list_sem.at[0]),
        pltpu.make_async_copy(cols_hbm, cols_s, list_sem.at[1]),
        pltpu.make_async_copy(cols_hbm, cols_v, list_sem.at[2]),
        pltpu.make_async_copy(rows_hbm, rows_v, list_sem.at[3]),
    ]

    for m in range(ch):
        mine_copy(m).start()
    for q in lists:
        q.start()
    for c in range(CHUNKS):
        tile_copy(c).start()

    barrier = pltpu.get_barrier_semaphore()
    for d in range(1, n_row):
        pl.semaphore_signal(barrier, inc=1, device_id={"row": (row + d) % n_row}, device_id_type=MESH)
    for d in range(1, n_col):
        pl.semaphore_signal(barrier, inc=1, device_id={"col": (col + d) % n_col}, device_id_type=MESH)
    for d in range(n_col):
        pl.semaphore_signal(barrier, inc=1, device_id={"col": (col + d) % n_col, "vec": oth}, device_id_type=MESH)
    pltpu.make_async_copy(x_mine, x_mine, mine_sem).wait()
    pl.semaphore_wait(barrier, n_row - 1 + 2 * n_col - 1)

    def remote(src, dst, send, recv, to):
        return pltpu.make_async_remote_copy(
            src_ref=src, dst_ref=dst, send_sem=send, recv_sem=recv, device_id=to, device_id_type=MESH
        )

    far = sorted(range(1, n_z), key=lambda d: -min(d, n_z - d))

    def owned(k):
        return pl.ds(k * ch, ch)

    def x_up(d):
        return remote(x_mine, x_col.at[owned(row)], x_s, xz_r, {"row": (row + 2 * d) % n_row})

    def x_side(d):
        return remote(x_mine, x_row.at[owned(col)], x_s, xr_r, {"col": (col + d) % n_col})

    def x_over(d):
        return remote(
            x_mine, x_oth.at[owned(col)], x_s, xo_r, {"col": (col + d) % n_col, "vec": oth}
        )

    for d in far:
        @pl.when(z + d < n_z)
        def _():
            x_up(d).start()
    for d in range(1, n_col):
        x_side(d).start()
    x_row[owned(col)] = x_mine[...]
    x_col[owned(row)] = x_mine[...]
    for k in range(2, n_row):
        @pl.when(k // 2 > z)
        def _():
            x_col[owned(k)] = jnp.zeros((ch, vloc, tile), BF16)
    for q in lists:
        q.wait()
    rows_l = rows_v[0]
    cols_l = cols_v[0]
    live = lax.broadcasted_iota(jnp.int32, (1, slots), 1) < count_v[0:1, 0:1]

    mate = {"row": row + 1 - 2 * core}

    def x_mate():
        return remote(x_mine, x_col.at[owned(row)], x_s, xf_r, mate)

    def x_forward(zz):
        part = x_col.at[owned(2 * zz + core)]
        return remote(part, part, x_s, xf_r, mate)

    x_mate().start()

    def bytes_of(ref, sem):
        pltpu.make_async_copy(ref, ref, sem).wait()

    def by_z(ref, unit, count, sem):
        for k in range(n_z):
            if count(k):
                @pl.when(z == k)
                def _():
                    bytes_of(ref.at[pl.ds(0, count(k) * unit)], sem)

    bytes_of(x_row.at[pl.ds(0, (n_col - 1) * ch)], xr_r)
    for d in range(n_col):
        x_over(d).start()

    zero = jnp.zeros((vloc, tile), BF16)

    def two(pick, first, out, trans):
        left = jnp.concatenate(
            [
                jnp.concatenate([pick(first), zero], 1),
                jnp.concatenate([zero, pick(first + 1)], 1),
            ],
            0,
        )
        w = jnp.concatenate([tiles[first], tiles[first + 1]], 1 if trans else 0)
        dims = (((1,), (1 if trans else 0,)), ((), ()))
        out[first * vloc:(first + 2) * vloc, :] = lax.dot_general(left, w, dims, preferred_element_type=F32)

    def pick_row(t):
        return x_row[rows_s[0, 0, t] & (span - 1)]

    def pick_col(t):
        c = cols_s[0, 0, t]
        return x_col[lax.shift_right_logical(c, span_bits) * ch + (c & (ch - 1))]

    bytes_of(tiles, tile_sem)
    for t in range(0, slots // 2, 2):
        two(pick_row, t, upper, False)

    by_z(x_col, ch, lambda k: k, xz_r)
    for d in far:
        @pl.when(z - d >= 0)
        def _():
            x_forward(z - d).start()

    for t in range(slots // 2, slots, 2):
        two(pick_row, t, upper, False)

    def scatter(src, hot, dst):
        m = hot.shape[0]
        for p in range(vloc // 2):
            both = jnp.concatenate(
                [src[pl.ds(2 * p, slots, stride=vloc), :], src[pl.ds(2 * p + 1, slots, stride=vloc), :]], 1
            )
            hi, lo = split_hi_lo(both)
            res = jnp.dot(hot, hi, preferred_element_type=F32) + jnp.dot(hot, lo, preferred_element_type=F32)
            dst[pl.ds(2 * p, m, stride=vloc), :] = res[:, :tile]
            dst[pl.ds(2 * p + 1, m, stride=vloc), :] = res[:, tile:]

    def one_hot(place, m):
        hit = lax.broadcasted_iota(jnp.int32, (m, slots), 0) == place
        return jnp.where(hit, 1.0, 0.0).astype(BF16)

    group = cols_l // span
    col_place = (group % 2) * (n_z * ch) + (group // 2) * ch + cols_l % ch
    scatter(upper, one_hot(jnp.where(live & (rows_l != cols_l), col_place, -1), n_row * ch), col_part)

    half = n_z * blk

    def z_block(zz):
        return pl.ds(pl.multiple_of(zz * blk, blk), blk)

    def swap(d):
        give = pl.ds(pl.multiple_of((1 - core) * half + (z - d) * blk, blk), blk)
        return remote(col_part.at[give], exch.at[z_block(z - d)], z_s, ex_r, mate)

    near = far + [0]
    for d in near:
        @pl.when(z - d >= 0)
        def _():
            swap(d).start()

    by_z(x_col, ch, lambda k: k + 1, xf_r)

    def z_send(d):
        return remote(
            z_acc.at[z_block(z - d)], z_recv.at[z], z_s, zs_r, {"row": row - 2 * d}
        )

    for t in range(0, slots, 2):
        if t == slots // 4:
            by_z(exch, blk, lambda k: k + 1, ex_r)
            for d in near:
                @pl.when(z - d >= 0)
                def _():
                    keep = pl.ds(pl.multiple_of(core * half + (z - d) * blk, blk), blk)
                    z_acc[z_block(z - d), :] = col_part[keep, :] + exch[z_block(z - d), :]
                    if d:
                        z_send(d).start()
        two(pick_col, t, down, True)

    row_hot = jnp.concatenate(
        [
            one_hot(jnp.where(live, rows_l % span, -1), span),
            one_hot(jnp.where(live & (rows_l == cols_l), rows_l % ch, -1), 2 * ch),
        ],
        0,
    )
    scatter(down, row_hot, row_part)

    def r_send(d):
        to = (col + d) % n_col
        return remote(
            row_part.at[pl.ds(pl.multiple_of(to * blk, blk), blk)], row_recv.at[col], o_s, rs_r,
            {"col": to},
        )

    bytes_of(x_oth, xo_r)

    def against(base, j):
        part = jnp.concatenate(
            [row_part[pl.ds(base + m * vloc, vloc), :] for m in range(ch)], 1
        )
        hi, lo = split_hi_lo(part)
        left = jnp.concatenate([hi, lo], 0)
        right = jnp.concatenate(
            [
                jnp.concatenate([x[j * ch + m] for m in range(ch)], 1)
                for x in (x_row, x_oth)
            ],
            0,
        )
        r = lax.dot_general(left, right, (((1,), (1,)), ((), ())), preferred_element_type=F32)
        return r[:vloc] + r[vloc:]

    whole = against(0, 0)
    for jj in range(1, n_col):
        whole = whole + against(jj * blk, jj)
    off = whole - against(span * vloc, col)
    pad = jnp.zeros((vloc, tile - 4 * vloc), F32)
    wide = jnp.concatenate([off, whole, pad], 1)
    packed = jnp.concatenate([wide[:1], wide[fold:fold + 1]], 0)
    for k in range(1, fold):
        pair = jnp.concatenate([wide[k:k + 1], wide[fold + k:fold + k + 1]], 0)
        packed = packed + pltpu.roll(pair, 4 * vloc * k, 1)
    g1_send[...] = packed
    g1_recv[vec * n_col + col] = packed

    def g1_side(d):
        return remote(g1_send, g1_recv.at[vec * n_col + col], o_s, g1_r, {"col": (col + d) % n_col})

    def g1_over(d):
        return remote(
            g1_send, g1_recv.at[vec * n_col + col], o_s, g1_r,
            {"col": (col + d) % n_col, "vec": oth},
        )

    for d in range(n_col):
        g1_over(d).start()
    for d in range(1, n_col):
        g1_side(d).start()
    for d in range(1, n_col):
        r_send(d).start()

    bytes_of(g1_recv.at[pl.ds(0, 2 * n_col - 1)], g1_r)
    own = g1_recv[vec * n_col]
    other = g1_recv[oth * n_col]
    for d in range(1, n_col):
        own = own + g1_recv[vec * n_col + d]
        other = other + g1_recv[oth * n_col + d]
    both = jnp.concatenate([own, other], 0)
    g2_send[...] = both
    g2_recv[row] = both

    def g2(d):
        return remote(g2_send, g2_recv.at[row], o_s, g2_r, {"row": (row + d) % n_row})

    order = sorted(range(1, n_row), key=lambda d: -min(d, n_row - d))
    for d in order:
        g2(d).start()

    bytes_of(row_recv.at[pl.ds(0, n_col - 1)], rs_r)
    image = row_part[pl.ds(pl.multiple_of(col * blk, blk), blk), :] + z_acc[z_block(z), :]
    for d in range(1, n_col):
        image = image + row_recv[(col + d) % n_col]
    acc[...] = image
    by_z(z_recv, 1, lambda k: n_z - 1 - k, zs_r)
    for d in range(n_z - 1, 0, -1):
        @pl.when(z + d < n_z)
        def _():
            acc[...] += z_recv[(z + d) % n_z]

    for m in range(ch):
        prod_ref[:, m * tile:(m + 1) * tile] = acc[m * vloc:(m + 1) * vloc, :].astype(BF16)

    bytes_of(g2_recv.at[pl.ds(0, n_row - 1)], g2_r)
    total = g2_recv[0]
    for d in range(1, n_row):
        total = total + g2_recv[d]

    def unpack(q):
        lines = [total[q:q + 2]] + [pltpu.roll(total[q:q + 2], tile - 4 * vloc * k, 1) for k in range(1, fold)]
        return jnp.concatenate([lines[k][p:p + 1] for p in range(2) for k in range(fold)], 0)

    mine = unpack(0)
    theirs = unpack(2)
    g_own = mine[:, 2 * vloc:3 * vloc] + jnp.transpose(mine)[:vloc, :vloc]
    g_oth = mine[:, 3 * vloc:4 * vloc] + jnp.transpose(theirs)[vloc:2 * vloc, :vloc]
    first = jnp.where(vec == 0, g_own, g_oth)
    second = jnp.where(vec == 0, g_oth, g_own)
    gram_ref[...] = jnp.concatenate([first, second], 1) * scale

    x_sends = n_z + 2 * n_col - 1
    bytes_of(upper.at[pl.ds(0, x_sends * blk // 2)], x_s)
    by_z(upper, blk, lambda k: 2 * k + 1, z_s)
    bytes_of(upper.at[pl.ds(0, (n_col - 1) * blk + (2 * n_col - 1) * 2 + (n_row - 1) * 4)], o_s)


def shards(n_row, n_col, vectors, tile_vals, tile_rows, tile_cols, tile_counts):
    vloc, width = vectors.shape
    slots, tile = tile_vals.shape[2], tile_vals.shape[3]
    ch = width // tile
    blk = ch * vloc
    n_z = n_row // 2
    dma = pltpu.SemaphoreType.DMA
    vmem = functools.partial(pl.BlockSpec, memory_space=pltpu.VMEM)
    scale = 1.0 / math.sqrt(width * n_row * n_col)
    counted = pltpu.with_memory_space_constraint(jnp.pad(tile_counts, ((0, 0), (0, tile - 1))), pltpu.VMEM)
    product, gram = pl.pallas_call(
        functools.partial(kernel, n_row, n_col, scale),
        out_shape=(
            pltpu.VMEM((vloc, width), BF16),
            pltpu.VMEM((vloc, 2 * vloc), F32),
        ),
        in_specs=[vmem()] + [pl.BlockSpec(memory_space=pltpu.HBM)] * 4,
        out_specs=(vmem(), vmem()),
        scratch_shapes=[
            pltpu.SMEM((1, 1, slots), jnp.int32),
            pltpu.SMEM((1, 1, slots), jnp.int32),
            pltpu.VMEM((1, 1, slots), jnp.int32),
            pltpu.VMEM((1, 1, slots), jnp.int32),
            pltpu.VMEM((slots, tile, tile), BF16),
            pltpu.VMEM((ch, vloc, tile), BF16),
            pltpu.VMEM((n_col * ch, vloc, tile), BF16),
            pltpu.VMEM((n_col * ch, vloc, tile), BF16),
            pltpu.VMEM((n_row * ch, vloc, tile), BF16),
            pltpu.VMEM((slots * vloc, tile), F32),
            pltpu.VMEM((slots * vloc, tile), F32),
            pltpu.VMEM((n_row * blk, tile), F32),
            pltpu.VMEM((n_z * blk, tile), F32),
            pltpu.VMEM((n_z * blk, tile), F32),
            pltpu.VMEM((n_z, blk, tile), F32),
            pltpu.VMEM(((n_col + 2) * blk, tile), F32),
            pltpu.VMEM((n_col, blk, tile), F32),
            pltpu.VMEM((blk, tile), F32),
            pltpu.VMEM((2, tile), F32),
            pltpu.VMEM((2 * n_col, 2, tile), F32),
            pltpu.VMEM((4, tile), F32),
            pltpu.VMEM((n_row, 4, tile), F32),
            dma((4,)), *([dma(())] * 14),
        ],
        compiler_params=pltpu.CompilerParams(
            collective_id=0, has_side_effects=True, vmem_limit_bytes=60 * 1024 * 1024
        ),
    )(counted, tile_rows, tile_cols, vectors, tile_vals)
    return product, gram.T


def solution(mesh):
    return jax.shard_map(
        functools.partial(shards, mesh.shape["row"], mesh.shape["col"]),
        mesh=mesh,
        in_specs=(
            P("vec", ("row", "col")),
            P("row", "col", None, None, None),
            P("row", "col", None),
            P("row", "col", None),
            P("row", "col"),
        ),
        out_specs=(P("vec", ("row", "col")), P(None, "vec")),
        check_vma=False,
    )
```

```python
import functools
import math

import jax
import jax.numpy as jnp
from jax import lax
from jax.experimental import pallas as pl
from jax.experimental.pallas import tpu as pltpu
from jax.sharding import PartitionSpec as P

MESH = pl.DeviceIdType.MESH
BF16 = jnp.bfloat16
F32 = jnp.float32
CHUNKS = 8


def split_hi_lo(value):
    hi = value.astype(BF16)
    lo = (value - hi.astype(F32)).astype(BF16)
    return hi, lo


def kernel(
    n_row, n_col, scale,
    count_v, rows_hbm, cols_hbm, x_ref, tiles_hbm,
    prod_ref, gram_ref,
    rows_s, cols_s, rows_v, cols_v, tiles, x_mine, x_row, x_oth, x_col, upper, down, col_part, exch, z_acc, z_recv, row_part, row_recv, acc,
    g1_send, g1_recv, g2_send, g2_recv,
    list_sem, mine_sem, tile_sem, x_s, xz_r, xf_r, xr_r, xp_r, xo_r, z_s, ex_r, zs_r, o_s, rs_r, g1_r, g2_r,
):
    n_z = n_row // 2
    slots = tiles.shape[0]
    tile = tiles.shape[1]
    vloc = x_ref.shape[0]
    ch = x_ref.shape[1] // tile
    blk = ch * vloc
    span = n_col * ch
    per = slots // CHUNKS
    fold = vloc // 2
    span_bits = span.bit_length() - 1
    row = lax.axis_index("row")
    col = lax.axis_index("col")
    vec = lax.axis_index("vec")
    z = row // 2
    core = row % 2
    oth = 1 - vec

    def tile_copy(c):
        part = pl.ds(c * per, per)
        return pltpu.make_async_copy(tiles_hbm.at[0, 0, part], tiles.at[part], tile_sem)

    def mine_copy(m):
        return pltpu.make_async_copy(x_ref.at[:, pl.ds(m * tile, tile)], x_mine.at[m], mine_sem)

    lists = [
        pltpu.make_async_copy(rows_hbm, rows_s, list_sem.at[0]),
        pltpu.make_async_copy(cols_hbm, cols_s, list_sem.at[1]),
        pltpu.make_async_copy(cols_hbm, cols_v, list_sem.at[2]),
        pltpu.make_async_copy(rows_hbm, rows_v, list_sem.at[3]),
    ]

    for m in range(ch):
        mine_copy(m).start()
    for q in lists:
        q.start()
    for c in range(CHUNKS):
        tile_copy(c).start()

    barrier = pltpu.get_barrier_semaphore()
    for d in range(1, n_row):
        pl.semaphore_signal(barrier, inc=1, device_id={"row": (row + d) % n_row}, device_id_type=MESH)
    for d in range(1, n_col):
        pl.semaphore_signal(barrier, inc=1, device_id={"col": (col + d) % n_col}, device_id_type=MESH)
    for d in range(n_col):
        pl.semaphore_signal(barrier, inc=1, device_id={"col": (col + d) % n_col, "vec": oth}, device_id_type=MESH)
    pltpu.make_async_copy(x_mine, x_mine, mine_sem).wait()
    pl.semaphore_wait(barrier, n_row - 1 + 2 * n_col - 1)

    def remote(src, dst, send, recv, to):
        return pltpu.make_async_remote_copy(
            src_ref=src, dst_ref=dst, send_sem=send, recv_sem=recv, device_id=to, device_id_type=MESH
        )

    far = sorted(range(1, n_z), key=lambda d: -min(d, n_z - d))

    def owned(k):
        return pl.ds(k * ch, ch)

    def x_up(d):
        return remote(x_mine, x_col.at[owned(row)], x_s, xz_r, {"row": (row + 2 * d) % n_row})

    def x_side(d):
        return remote(x_mine, x_row.at[owned(col)], x_s, xr_r, {"col": (col + d) % n_col})

    def x_over():
        return remote(x_mine, x_oth.at[owned(col)], x_s, xp_r, {"vec": oth})

    def x_pass(d):
        part = x_oth.at[owned(col)]
        return remote(part, part, x_s, xo_r, {"col": (col + d) % n_col})

    for d in far:
        @pl.when(z + d < n_z)
        def _():
            x_up(d).start()
    for d in range(1, n_col):
        x_side(d).start()
    x_over().start()
    x_row[owned(col)] = x_mine[...]
    x_col[owned(row)] = x_mine[...]
    for k in range(2, n_row):
        @pl.when(k // 2 > z)
        def _():
            x_col[owned(k)] = jnp.zeros((ch, vloc, tile), BF16)
    for q in lists:
        q.wait()
    rows_l = rows_v[0]
    cols_l = cols_v[0]
    live = lax.broadcasted_iota(jnp.int32, (1, slots), 1) < count_v[0:1, 0:1]

    mate = {"row": row + 1 - 2 * core}

    def x_mate():
        return remote(x_mine, x_col.at[owned(row)], x_s, xf_r, mate)

    def x_forward(zz):
        part = x_col.at[owned(2 * zz + core)]
        return remote(part, part, x_s, xf_r, mate)

    x_mate().start()

    def bytes_of(ref, sem):
        pltpu.make_async_copy(ref, ref, sem).wait()

    def by_z(ref, unit, count, sem):
        for k in range(n_z):
            if count(k):
                @pl.when(z == k)
                def _():
                    bytes_of(ref.at[pl.ds(0, count(k) * unit)], sem)

    bytes_of(x_row.at[pl.ds(0, (n_col - 1) * ch)], xr_r)
    bytes_of(x_oth.at[owned(col)], xp_r)
    for d in range(1, n_col):
        x_pass(d).start()

    zero = jnp.zeros((vloc, tile), BF16)

    def two(pick, first, out, trans):
        left = jnp.concatenate(
            [
                jnp.concatenate([pick(first), zero], 1),
                jnp.concatenate([zero, pick(first + 1)], 1),
            ],
            0,
        )
        w = jnp.concatenate([tiles[first], tiles[first + 1]], 1 if trans else 0)
        dims = (((1,), (1 if trans else 0,)), ((), ()))
        out[first * vloc:(first + 2) * vloc, :] = lax.dot_general(left, w, dims, preferred_element_type=F32)

    def pick_row(t):
        return x_row[rows_s[0, 0, t] & (span - 1)]

    def pick_col(t):
        c = cols_s[0, 0, t]
        return x_col[lax.shift_right_logical(c, span_bits) * ch + (c & (ch - 1))]

    bytes_of(tiles, tile_sem)
    for t in range(0, 3 * slots // 4, 2):
        two(pick_row, t, upper, False)

    by_z(x_col, ch, lambda k: k, xz_r)
    for d in far:
        @pl.when(z - d >= 0)
        def _():
            x_forward(z - d).start()

    for t in range(3 * slots // 4, slots, 2):
        two(pick_row, t, upper, False)

    def scatter(src, hot, dst):
        m = hot.shape[0]
        for p in range(vloc // 2):
            both = jnp.concatenate(
                [src[pl.ds(2 * p, slots, stride=vloc), :], src[pl.ds(2 * p + 1, slots, stride=vloc), :]], 1
            )
            hi, lo = split_hi_lo(both)
            res = jnp.dot(hot, hi, preferred_element_type=F32) + jnp.dot(hot, lo, preferred_element_type=F32)
            dst[pl.ds(2 * p, m, stride=vloc), :] = res[:, :tile]
            dst[pl.ds(2 * p + 1, m, stride=vloc), :] = res[:, tile:]

    def one_hot(place, m):
        hit = lax.broadcasted_iota(jnp.int32, (m, slots), 0) == place
        return jnp.where(hit, 1.0, 0.0).astype(BF16)

    group = cols_l // span
    col_place = (group % 2) * (n_z * ch) + (group // 2) * ch + cols_l % ch
    scatter(upper, one_hot(jnp.where(live & (rows_l != cols_l), col_place, -1), n_row * ch), col_part)

    half = n_z * blk

    def z_block(zz):
        return pl.ds(pl.multiple_of(zz * blk, blk), blk)

    def swap(d):
        give = pl.ds(pl.multiple_of((1 - core) * half + (z - d) * blk, blk), blk)
        return remote(col_part.at[give], exch.at[z_block(z - d)], z_s, ex_r, mate)

    near = far + [0]
    for d in near:
        @pl.when(z - d >= 0)
        def _():
            swap(d).start()

    by_z(x_col, ch, lambda k: k + 1, xf_r)

    def z_send(d):
        return remote(
            z_acc.at[z_block(z - d)], z_recv.at[z], z_s, zs_r, {"row": row - 2 * d}
        )

    for t in range(0, slots, 2):
        if t == slots // 2:
            by_z(exch, blk, lambda k: k + 1, ex_r)
            for d in near:
                @pl.when(z - d >= 0)
                def _():
                    keep = pl.ds(pl.multiple_of(core * half + (z - d) * blk, blk), blk)
                    z_acc[z_block(z - d), :] = col_part[keep, :] + exch[z_block(z - d), :]
                    if d:
                        z_send(d).start()
        two(pick_col, t, down, True)

    row_hot = jnp.concatenate(
        [
            one_hot(jnp.where(live, rows_l % span, -1), span),
            one_hot(jnp.where(live & (rows_l == cols_l), rows_l % ch, -1), 2 * ch),
        ],
        0,
    )
    scatter(down, row_hot, row_part)

    def r_send(d):
        to = (col + d) % n_col
        return remote(
            row_part.at[pl.ds(pl.multiple_of(to * blk, blk), blk)], row_recv.at[col], o_s, rs_r,
            {"col": to},
        )

    bytes_of(x_oth.at[pl.ds(0, (n_col - 1) * ch)], xo_r)

    def against(base, j):
        part = jnp.concatenate(
            [row_part[pl.ds(base + m * vloc, vloc), :] for m in range(ch)], 1
        )
        hi, lo = split_hi_lo(part)
        left = jnp.concatenate([hi, lo], 0)
        right = jnp.concatenate(
            [
                jnp.concatenate([x[j * ch + m] for m in range(ch)], 1)
                for x in (x_row, x_oth)
            ],
            0,
        )
        r = lax.dot_general(left, right, (((1,), (1,)), ((), ())), preferred_element_type=F32)
        return r[:vloc] + r[vloc:]

    whole = against(0, 0)
    for jj in range(1, n_col):
        whole = whole + against(jj * blk, jj)
    off = whole - against(span * vloc, col)
    pad = jnp.zeros((vloc, tile - 4 * vloc), F32)
    wide = jnp.concatenate([off, whole, pad], 1)
    packed = jnp.concatenate([wide[:1], wide[fold:fold + 1]], 0)
    for k in range(1, fold):
        pair = jnp.concatenate([wide[k:k + 1], wide[fold + k:fold + k + 1]], 0)
        packed = packed + pltpu.roll(pair, 4 * vloc * k, 1)
    g1_send[...] = packed
    g1_recv[vec * n_col + col] = packed

    def g1_side(d):
        return remote(g1_send, g1_recv.at[vec * n_col + col], o_s, g1_r, {"col": (col + d) % n_col})

    def g1_over(d):
        return remote(
            g1_send, g1_recv.at[vec * n_col + col], o_s, g1_r,
            {"col": (col + d) % n_col, "vec": oth},
        )

    for d in range(n_col):
        g1_over(d).start()
    for d in range(1, n_col):
        g1_side(d).start()
    for d in range(1, n_col):
        r_send(d).start()

    bytes_of(g1_recv.at[pl.ds(0, 2 * n_col - 1)], g1_r)
    own = g1_recv[vec * n_col]
    other = g1_recv[oth * n_col]
    for d in range(1, n_col):
        own = own + g1_recv[vec * n_col + d]
        other = other + g1_recv[oth * n_col + d]
    both = jnp.concatenate([own, other], 0)
    g2_send[...] = both
    g2_recv[row] = both

    def g2(d):
        return remote(g2_send, g2_recv.at[row], o_s, g2_r, {"row": (row + d) % n_row})

    order = sorted(range(1, n_row), key=lambda d: -min(d, n_row - d))
    for d in order:
        g2(d).start()

    bytes_of(row_recv.at[pl.ds(0, n_col - 1)], rs_r)
    image = row_part[pl.ds(pl.multiple_of(col * blk, blk), blk), :] + z_acc[z_block(z), :]
    for d in range(1, n_col):
        image = image + row_recv[(col + d) % n_col]
    acc[...] = image
    by_z(z_recv, 1, lambda k: n_z - 1 - k, zs_r)
    for d in range(n_z - 1, 0, -1):
        @pl.when(z + d < n_z)
        def _():
            acc[...] += z_recv[(z + d) % n_z]

    for m in range(ch):
        prod_ref[:, m * tile:(m + 1) * tile] = acc[m * vloc:(m + 1) * vloc, :].astype(BF16)

    bytes_of(g2_recv.at[pl.ds(0, n_row - 1)], g2_r)
    total = g2_recv[0]
    for d in range(1, n_row):
        total = total + g2_recv[d]

    def unpack(q):
        lines = [total[q:q + 2]] + [pltpu.roll(total[q:q + 2], tile - 4 * vloc * k, 1) for k in range(1, fold)]
        return jnp.concatenate([lines[k][p:p + 1] for p in range(2) for k in range(fold)], 0)

    mine = unpack(0)
    theirs = unpack(2)
    g_own = mine[:, 2 * vloc:3 * vloc] + jnp.transpose(mine)[:vloc, :vloc]
    g_oth = mine[:, 3 * vloc:4 * vloc] + jnp.transpose(theirs)[vloc:2 * vloc, :vloc]
    first = jnp.where(vec == 0, g_own, g_oth)
    second = jnp.where(vec == 0, g_oth, g_own)
    gram_ref[...] = jnp.concatenate([first, second], 1) * scale

    x_sends = n_z + 2 * n_col - 1
    bytes_of(upper.at[pl.ds(0, x_sends * blk // 2)], x_s)
    by_z(upper, blk, lambda k: 2 * k + 1, z_s)
    bytes_of(upper.at[pl.ds(0, (n_col - 1) * blk + (2 * n_col - 1) * 2 + (n_row - 1) * 4)], o_s)


def hand_over(prod_ref, gram_ref, prod_out, gram_out, sem):
    one = pltpu.make_async_copy(prod_ref, prod_out, sem.at[0])
    two = pltpu.make_async_copy(gram_ref, gram_out, sem.at[1])
    one.start()
    two.start()
    one.wait()
    two.wait()


def shards(n_row, n_col, vectors, tile_vals, tile_rows, tile_cols, tile_counts):
    vloc, width = vectors.shape
    slots, tile = tile_vals.shape[2], tile_vals.shape[3]
    ch = width // tile
    blk = ch * vloc
    n_z = n_row // 2
    dma = pltpu.SemaphoreType.DMA
    vmem = functools.partial(pl.BlockSpec, memory_space=pltpu.VMEM)
    scale = 1.0 / math.sqrt(width * n_row * n_col)
    counted = pltpu.with_memory_space_constraint(jnp.pad(tile_counts, ((0, 0), (0, tile - 1))), pltpu.VMEM)
    product, gram = pl.pallas_call(
        functools.partial(kernel, n_row, n_col, scale),
        out_shape=(
            pltpu.VMEM((vloc, width), BF16),
            pltpu.VMEM((vloc, 2 * vloc), F32),
        ),
        in_specs=[vmem()] + [pl.BlockSpec(memory_space=pltpu.HBM)] * 4,
        out_specs=(vmem(), vmem()),
        scratch_shapes=[
            pltpu.SMEM((1, 1, slots), jnp.int32),
            pltpu.SMEM((1, 1, slots), jnp.int32),
            pltpu.VMEM((1, 1, slots), jnp.int32),
            pltpu.VMEM((1, 1, slots), jnp.int32),
            pltpu.VMEM((slots, tile, tile), BF16),
            pltpu.VMEM((ch, vloc, tile), BF16),
            pltpu.VMEM((n_col * ch, vloc, tile), BF16),
            pltpu.VMEM((n_col * ch, vloc, tile), BF16),
            pltpu.VMEM((n_row * ch, vloc, tile), BF16),
            pltpu.VMEM((slots * vloc, tile), F32),
            pltpu.VMEM((slots * vloc, tile), F32),
            pltpu.VMEM((n_row * blk, tile), F32),
            pltpu.VMEM((n_z * blk, tile), F32),
            pltpu.VMEM((n_z * blk, tile), F32),
            pltpu.VMEM((n_z, blk, tile), F32),
            pltpu.VMEM(((n_col + 2) * blk, tile), F32),
            pltpu.VMEM((n_col, blk, tile), F32),
            pltpu.VMEM((blk, tile), F32),
            pltpu.VMEM((2, tile), F32),
            pltpu.VMEM((2 * n_col, 2, tile), F32),
            pltpu.VMEM((4, tile), F32),
            pltpu.VMEM((n_row, 4, tile), F32),
            dma((4,)), *([dma(())] * 15),
        ],
        compiler_params=pltpu.CompilerParams(
            collective_id=0, has_side_effects=True, vmem_limit_bytes=60 * 1024 * 1024
        ),
    )(counted, tile_rows, tile_cols, vectors, tile_vals)
    product, gram = pl.pallas_call(
        hand_over,
        out_shape=(
            jax.ShapeDtypeStruct((vloc, width), BF16),
            jax.ShapeDtypeStruct((vloc, 2 * vloc), F32),
        ),
        in_specs=[vmem(), vmem()],
        out_specs=(pl.BlockSpec(memory_space=pl.ANY), pl.BlockSpec(memory_space=pl.ANY)),
        scratch_shapes=[dma((2,))],
    )(pltpu.with_memory_space_constraint(product, pltpu.VMEM), pltpu.with_memory_space_constraint(gram, pltpu.VMEM))
    return product, gram.T


def solution(mesh):
    return jax.shard_map(
        functools.partial(shards, mesh.shape["row"], mesh.shape["col"]),
        mesh=mesh,
        in_specs=(
            P("vec", ("row", "col")),
            P("row", "col", None, None, None),
            P("row", "col", None),
            P("row", "col", None),
            P("row", "col"),
        ),
        out_specs=(P("vec", ("row", "col")), P(None, "vec")),
        check_vma=False,
    )
```

```python
import functools
import math

import jax
import jax.numpy as jnp
from jax import lax
from jax.experimental import pallas as pl
from jax.experimental.pallas import tpu as pltpu
from jax.sharding import PartitionSpec as P

MESH = pl.DeviceIdType.MESH
BF16 = jnp.bfloat16
F32 = jnp.float32
CHUNKS = 8


def split_hi_lo(value):
    hi = value.astype(BF16)
    lo = (value - hi.astype(F32)).astype(BF16)
    return hi, lo


def kernel(
    n_row, n_col, scale,
    count_v, rows_hbm, cols_hbm, x_ref, tiles_hbm,
    prod_ref, gram_ref,
    rows_s, cols_s, rows_v, cols_v, tiles, x_mine, x_row, x_oth, x_col, upper, down, col_part, exch, z_acc, z_recv, row_part, row_recv, acc,
    g1_send, g1_recv, g2_send, g2_recv,
    list_sem, mine_sem, tile_sem, x_s, xz_r, xf_r, xr_r, xp_r, xo_r, z_s, ex_r, zs_r, o_s, rs_r, g1_r, g2_r,
):
    n_z = n_row // 2
    slots = tiles.shape[0]
    tile = tiles.shape[1]
    vloc = x_ref.shape[0]
    ch = x_ref.shape[1] // tile
    blk = ch * vloc
    span = n_col * ch
    per = slots // CHUNKS
    fold = vloc // 2
    span_bits = span.bit_length() - 1
    row = lax.axis_index("row")
    col = lax.axis_index("col")
    vec = lax.axis_index("vec")
    z = row // 2
    core = row % 2
    oth = 1 - vec

    def tile_copy(c):
        part = pl.ds(c * per, per)
        return pltpu.make_async_copy(tiles_hbm.at[0, 0, part], tiles.at[part], tile_sem)

    def mine_copy(m):
        return pltpu.make_async_copy(x_ref.at[:, pl.ds(m * tile, tile)], x_mine.at[m], mine_sem)

    lists = [
        pltpu.make_async_copy(rows_hbm, rows_s, list_sem.at[0]),
        pltpu.make_async_copy(cols_hbm, cols_s, list_sem.at[1]),
        pltpu.make_async_copy(cols_hbm, cols_v, list_sem.at[2]),
        pltpu.make_async_copy(rows_hbm, rows_v, list_sem.at[3]),
    ]

    for m in range(ch):
        mine_copy(m).start()
    for q in lists:
        q.start()
    for c in range(CHUNKS):
        tile_copy(c).start()

    barrier = pltpu.get_barrier_semaphore()
    for d in range(1, n_row):
        pl.semaphore_signal(barrier, inc=1, device_id={"row": (row + d) % n_row}, device_id_type=MESH)
    for d in range(1, n_col):
        pl.semaphore_signal(barrier, inc=1, device_id={"col": (col + d) % n_col}, device_id_type=MESH)
    for d in range(n_col):
        pl.semaphore_signal(barrier, inc=1, device_id={"col": (col + d) % n_col, "vec": oth}, device_id_type=MESH)
    pltpu.make_async_copy(x_mine, x_mine, mine_sem).wait()
    pl.semaphore_wait(barrier, n_row - 1 + 2 * n_col - 1)

    def remote(src, dst, send, recv, to):
        return pltpu.make_async_remote_copy(
            src_ref=src, dst_ref=dst, send_sem=send, recv_sem=recv, device_id=to, device_id_type=MESH
        )

    far = sorted(range(1, n_z), key=lambda d: -min(d, n_z - d))

    def owned(k):
        return pl.ds(k * ch, ch)

    def x_up(d):
        return remote(x_mine, x_col.at[owned(row)], x_s, xz_r, {"row": (row + 2 * d) % n_row})

    def x_side(d):
        return remote(x_mine, x_row.at[owned(col)], x_s, xr_r, {"col": (col + d) % n_col})

    def x_over():
        return remote(x_mine, x_oth.at[owned(col)], x_s, xp_r, {"vec": oth})

    def x_pass(d):
        part = x_oth.at[owned(col)]
        return remote(part, part, x_s, xo_r, {"col": (col + d) % n_col})

    for d in far:
        @pl.when(z + d < n_z)
        def _():
            x_up(d).start()
    for d in range(1, n_col):
        x_side(d).start()
    x_over().start()
    x_row[owned(col)] = x_mine[...]
    x_col[owned(row)] = x_mine[...]
    for k in range(2, n_row):
        @pl.when(k // 2 > z)
        def _():
            x_col[owned(k)] = jnp.zeros((ch, vloc, tile), BF16)
    for q in lists:
        q.wait()
    rows_l = rows_v[0]
    cols_l = cols_v[0]
    live = lax.broadcasted_iota(jnp.int32, (1, slots), 1) < count_v[0:1, 0:1]

    mate = {"row": row + 1 - 2 * core}

    def x_mate():
        return remote(x_mine, x_col.at[owned(row)], x_s, xf_r, mate)

    def x_forward(zz):
        part = x_col.at[owned(2 * zz + core)]
        return remote(part, part, x_s, xf_r, mate)

    x_mate().start()

    def bytes_of(ref, sem):
        pltpu.make_async_copy(ref, ref, sem).wait()

    def by_z(ref, unit, count, sem):
        for k in range(n_z):
            if count(k):
                @pl.when(z == k)
                def _():
                    bytes_of(ref.at[pl.ds(0, count(k) * unit)], sem)

    bytes_of(x_row.at[pl.ds(0, (n_col - 1) * ch)], xr_r)
    bytes_of(x_oth.at[owned(col)], xp_r)
    for d in range(1, n_col):
        x_pass(d).start()

    zero = jnp.zeros((vloc, tile), BF16)

    def two(pick, first, out, trans):
        left = jnp.concatenate(
            [
                jnp.concatenate([pick(first), zero], 1),
                jnp.concatenate([zero, pick(first + 1)], 1),
            ],
            0,
        )
        w = jnp.concatenate([tiles[first], tiles[first + 1]], 1 if trans else 0)
        dims = (((1,), (1 if trans else 0,)), ((), ()))
        out[first * vloc:(first + 2) * vloc, :] = lax.dot_general(left, w, dims, preferred_element_type=F32)

    def pick_row(t):
        return x_row[rows_s[0, 0, t] & (span - 1)]

    def pick_col(t):
        c = cols_s[0, 0, t]
        return x_col[lax.shift_right_logical(c, span_bits) * ch + (c & (ch - 1))]

    bytes_of(tiles, tile_sem)
    for t in range(0, slots, 2):
        two(pick_row, t, upper, False)

    by_z(x_col, ch, lambda k: k, xz_r)
    for d in far:
        @pl.when(z - d >= 0)
        def _():
            x_forward(z - d).start()

    for t in range(slots, slots, 2):
        two(pick_row, t, upper, False)

    def scatter(src, hot, dst):
        m = hot.shape[0]
        for p in range(vloc // 2):
            both = jnp.concatenate(
                [src[pl.ds(2 * p, slots, stride=vloc), :], src[pl.ds(2 * p + 1, slots, stride=vloc), :]], 1
            )
            hi, lo = split_hi_lo(both)
            res = jnp.dot(hot, hi, preferred_element_type=F32) + jnp.dot(hot, lo, preferred_element_type=F32)
            dst[pl.ds(2 * p, m, stride=vloc), :] = res[:, :tile]
            dst[pl.ds(2 * p + 1, m, stride=vloc), :] = res[:, tile:]

    def one_hot(place, m):
        hit = lax.broadcasted_iota(jnp.int32, (m, slots), 0) == place
        return jnp.where(hit, 1.0, 0.0).astype(BF16)

    group = cols_l // span
    col_place = (group % 2) * (n_z * ch) + (group // 2) * ch + cols_l % ch
    scatter(upper, one_hot(jnp.where(live & (rows_l != cols_l), col_place, -1), n_row * ch), col_part)

    half = n_z * blk

    def z_block(zz):
        return pl.ds(pl.multiple_of(zz * blk, blk), blk)

    def swap(d):
        give = pl.ds(pl.multiple_of((1 - core) * half + (z - d) * blk, blk), blk)
        return remote(col_part.at[give], exch.at[z_block(z - d)], z_s, ex_r, mate)

    near = far + [0]
    for d in near:
        @pl.when(z - d >= 0)
        def _():
            swap(d).start()

    by_z(x_col, ch, lambda k: k + 1, xf_r)

    def z_send(d):
        return remote(
            z_acc.at[z_block(z - d)], z_recv.at[z], z_s, zs_r, {"row": row - 2 * d}
        )

    for t in range(0, slots, 2):
        two(pick_col, t, down, True)

    by_z(exch, blk, lambda k: k + 1, ex_r)
    for d in near:
        @pl.when(z - d >= 0)
        def _():
            keep = pl.ds(pl.multiple_of(core * half + (z - d) * blk, blk), blk)
            z_acc[z_block(z - d), :] = col_part[keep, :] + exch[z_block(z - d), :]
            if d:
                z_send(d).start()


    row_hot = jnp.concatenate(
        [
            one_hot(jnp.where(live, rows_l % span, -1), span),
            one_hot(jnp.where(live & (rows_l == cols_l), rows_l % ch, -1), 2 * ch),
        ],
        0,
    )
    scatter(down, row_hot, row_part)

    def r_send(d):
        to = (col + d) % n_col
        return remote(
            row_part.at[pl.ds(pl.multiple_of(to * blk, blk), blk)], row_recv.at[col], o_s, rs_r,
            {"col": to},
        )

    bytes_of(x_oth.at[pl.ds(0, (n_col - 1) * ch)], xo_r)

    def against(base, j):
        part = jnp.concatenate(
            [row_part[pl.ds(base + m * vloc, vloc), :] for m in range(ch)], 1
        )
        hi, lo = split_hi_lo(part)
        left = jnp.concatenate([hi, lo], 0)
        right = jnp.concatenate(
            [
                jnp.concatenate([x[j * ch + m] for m in range(ch)], 1)
                for x in (x_row, x_oth)
            ],
            0,
        )
        r = lax.dot_general(left, right, (((1,), (1,)), ((), ())), preferred_element_type=F32)
        return r[:vloc] + r[vloc:]

    whole = against(0, 0)
    for jj in range(1, n_col):
        whole = whole + against(jj * blk, jj)
    off = whole - against(span * vloc, col)
    pad = jnp.zeros((vloc, tile - 4 * vloc), F32)
    wide = jnp.concatenate([off, whole, pad], 1)
    packed = jnp.concatenate([wide[:1], wide[fold:fold + 1]], 0)
    for k in range(1, fold):
        pair = jnp.concatenate([wide[k:k + 1], wide[fold + k:fold + k + 1]], 0)
        packed = packed + pltpu.roll(pair, 4 * vloc * k, 1)
    g1_send[...] = packed
    g1_recv[vec * n_col + col] = packed

    def g1_side(d):
        return remote(g1_send, g1_recv.at[vec * n_col + col], o_s, g1_r, {"col": (col + d) % n_col})

    def g1_over(d):
        return remote(
            g1_send, g1_recv.at[vec * n_col + col], o_s, g1_r,
            {"col": (col + d) % n_col, "vec": oth},
        )

    for d in range(n_col):
        g1_over(d).start()
    for d in range(1, n_col):
        g1_side(d).start()
    for d in range(1, n_col):
        r_send(d).start()

    bytes_of(g1_recv.at[pl.ds(0, 2 * n_col - 1)], g1_r)
    own = g1_recv[vec * n_col]
    other = g1_recv[oth * n_col]
    for d in range(1, n_col):
        own = own + g1_recv[vec * n_col + d]
        other = other + g1_recv[oth * n_col + d]
    both = jnp.concatenate([own, other], 0)
    g2_send[...] = both
    g2_recv[row] = both

    def g2(d):
        return remote(g2_send, g2_recv.at[row], o_s, g2_r, {"row": (row + d) % n_row})

    order = sorted(range(1, n_row), key=lambda d: -min(d, n_row - d))
    for d in order:
        g2(d).start()

    bytes_of(row_recv.at[pl.ds(0, n_col - 1)], rs_r)
    image = row_part[pl.ds(pl.multiple_of(col * blk, blk), blk), :] + z_acc[z_block(z), :]
    for d in range(1, n_col):
        image = image + row_recv[(col + d) % n_col]
    acc[...] = image
    by_z(z_recv, 1, lambda k: n_z - 1 - k, zs_r)
    for d in range(n_z - 1, 0, -1):
        @pl.when(z + d < n_z)
        def _():
            acc[...] += z_recv[(z + d) % n_z]

    for m in range(ch):
        prod_ref[:, m * tile:(m + 1) * tile] = acc[m * vloc:(m + 1) * vloc, :].astype(BF16)

    bytes_of(g2_recv.at[pl.ds(0, n_row - 1)], g2_r)
    total = g2_recv[0]
    for d in range(1, n_row):
        total = total + g2_recv[d]

    def unpack(q):
        lines = [total[q:q + 2]] + [pltpu.roll(total[q:q + 2], tile - 4 * vloc * k, 1) for k in range(1, fold)]
        return jnp.concatenate([lines[k][p:p + 1] for p in range(2) for k in range(fold)], 0)

    mine = unpack(0)
    theirs = unpack(2)
    g_own = mine[:, 2 * vloc:3 * vloc] + jnp.transpose(mine)[:vloc, :vloc]
    g_oth = mine[:, 3 * vloc:4 * vloc] + jnp.transpose(theirs)[vloc:2 * vloc, :vloc]
    first = jnp.where(vec == 0, g_own, g_oth)
    second = jnp.where(vec == 0, g_oth, g_own)
    gram_ref[...] = jnp.concatenate([first, second], 1) * scale

    x_sends = n_z + 2 * n_col - 1
    bytes_of(upper.at[pl.ds(0, x_sends * blk // 2)], x_s)
    by_z(upper, blk, lambda k: 2 * k + 1, z_s)
    bytes_of(upper.at[pl.ds(0, (n_col - 1) * blk + (2 * n_col - 1) * 2 + (n_row - 1) * 4)], o_s)


def hand_over(prod_ref, gram_ref, prod_out, gram_out, sem):
    one = pltpu.make_async_copy(prod_ref, prod_out, sem.at[0])
    two = pltpu.make_async_copy(gram_ref, gram_out, sem.at[1])
    one.start()
    two.start()
    one.wait()
    two.wait()


def shards(n_row, n_col, vectors, tile_vals, tile_rows, tile_cols, tile_counts):
    vloc, width = vectors.shape
    slots, tile = tile_vals.shape[2], tile_vals.shape[3]
    ch = width // tile
    blk = ch * vloc
    n_z = n_row // 2
    dma = pltpu.SemaphoreType.DMA
    vmem = functools.partial(pl.BlockSpec, memory_space=pltpu.VMEM)
    scale = 1.0 / math.sqrt(width * n_row * n_col)
    counted = pltpu.with_memory_space_constraint(jnp.pad(tile_counts, ((0, 0), (0, tile - 1))), pltpu.VMEM)
    product, gram = pl.pallas_call(
        functools.partial(kernel, n_row, n_col, scale),
        out_shape=(
            pltpu.VMEM((vloc, width), BF16),
            pltpu.VMEM((vloc, 2 * vloc), F32),
        ),
        in_specs=[vmem()] + [pl.BlockSpec(memory_space=pltpu.HBM)] * 4,
        out_specs=(vmem(), vmem()),
        scratch_shapes=[
            pltpu.SMEM((1, 1, slots), jnp.int32),
            pltpu.SMEM((1, 1, slots), jnp.int32),
            pltpu.VMEM((1, 1, slots), jnp.int32),
            pltpu.VMEM((1, 1, slots), jnp.int32),
            pltpu.VMEM((slots, tile, tile), BF16),
            pltpu.VMEM((ch, vloc, tile), BF16),
            pltpu.VMEM((n_col * ch, vloc, tile), BF16),
            pltpu.VMEM((n_col * ch, vloc, tile), BF16),
            pltpu.VMEM((n_row * ch, vloc, tile), BF16),
            pltpu.VMEM((slots * vloc, tile), F32),
            pltpu.VMEM((slots * vloc, tile), F32),
            pltpu.VMEM((n_row * blk, tile), F32),
            pltpu.VMEM((n_z * blk, tile), F32),
            pltpu.VMEM((n_z * blk, tile), F32),
            pltpu.VMEM((n_z, blk, tile), F32),
            pltpu.VMEM(((n_col + 2) * blk, tile), F32),
            pltpu.VMEM((n_col, blk, tile), F32),
            pltpu.VMEM((blk, tile), F32),
            pltpu.VMEM((2, tile), F32),
            pltpu.VMEM((2 * n_col, 2, tile), F32),
            pltpu.VMEM((4, tile), F32),
            pltpu.VMEM((n_row, 4, tile), F32),
            dma((4,)), *([dma(())] * 15),
        ],
        compiler_params=pltpu.CompilerParams(
            collective_id=0, has_side_effects=True, vmem_limit_bytes=60 * 1024 * 1024
        ),
    )(counted, tile_rows, tile_cols, vectors, tile_vals)
    product, gram = pl.pallas_call(
        hand_over,
        out_shape=(
            jax.ShapeDtypeStruct((vloc, width), BF16),
            jax.ShapeDtypeStruct((vloc, 2 * vloc), F32),
        ),
        in_specs=[vmem(), vmem()],
        out_specs=(pl.BlockSpec(memory_space=pl.ANY), pl.BlockSpec(memory_space=pl.ANY)),
        scratch_shapes=[dma((2,))],
    )(pltpu.with_memory_space_constraint(product, pltpu.VMEM), pltpu.with_memory_space_constraint(gram, pltpu.VMEM))
    return product, gram.T


def solution(mesh):
    return jax.shard_map(
        functools.partial(shards, mesh.shape["row"], mesh.shape["col"]),
        mesh=mesh,
        in_specs=(
            P("vec", ("row", "col")),
            P("row", "col", None, None, None),
            P("row", "col", None),
            P("row", "col", None),
            P("row", "col"),
        ),
        out_specs=(P("vec", ("row", "col")), P(None, "vec")),
        check_vma=False,
    )
```

```python
import functools
import math

import jax
import jax.numpy as jnp
from jax import lax
from jax.experimental import pallas as pl
from jax.experimental.pallas import tpu as pltpu
from jax.sharding import PartitionSpec as P

MESH = pl.DeviceIdType.MESH
BF16 = jnp.bfloat16
F32 = jnp.float32
CHUNKS = 8


def split_hi_lo(value):
    hi = value.astype(BF16)
    lo = (value - hi.astype(F32)).astype(BF16)
    return hi, lo


def kernel(
    n_row, n_col, scale,
    count_v, rows_hbm, cols_hbm, x_ref, tiles_hbm,
    prod_ref, gram_ref,
    rows_s, cols_s, rows_v, cols_v, tiles, flipped, x_mine, x_row, x_oth, x_col, upper, down, col_part, exch, z_acc, z_recv, row_part, row_recv, acc,
    g1_send, g1_recv, g2_send, g2_recv,
    list_sem, mine_sem, tile_sem, x_s, xz_r, xf_r, xr_r, xp_r, xo_r, z_s, ex_r, zs_r, o_s, rs_r, g1_r, g2_r,
):
    n_z = n_row // 2
    slots = tiles.shape[0]
    tile = tiles.shape[1]
    vloc = x_ref.shape[0]
    ch = x_ref.shape[1] // tile
    blk = ch * vloc
    span = n_col * ch
    per = slots // CHUNKS
    fold = vloc // 2
    span_bits = span.bit_length() - 1
    row = lax.axis_index("row")
    col = lax.axis_index("col")
    vec = lax.axis_index("vec")
    z = row // 2
    core = row % 2
    oth = 1 - vec

    def tile_copy(c):
        part = pl.ds(c * per, per)
        return pltpu.make_async_copy(tiles_hbm.at[0, 0, part], tiles.at[part], tile_sem)

    def mine_copy(m):
        return pltpu.make_async_copy(x_ref.at[:, pl.ds(m * tile, tile)], x_mine.at[m], mine_sem)

    lists = [
        pltpu.make_async_copy(rows_hbm, rows_s, list_sem.at[0]),
        pltpu.make_async_copy(cols_hbm, cols_s, list_sem.at[1]),
        pltpu.make_async_copy(cols_hbm, cols_v, list_sem.at[2]),
        pltpu.make_async_copy(rows_hbm, rows_v, list_sem.at[3]),
    ]

    for m in range(ch):
        mine_copy(m).start()
    for q in lists:
        q.start()
    for c in range(CHUNKS):
        tile_copy(c).start()

    barrier = pltpu.get_barrier_semaphore()
    for d in range(1, n_row):
        pl.semaphore_signal(barrier, inc=1, device_id={"row": (row + d) % n_row}, device_id_type=MESH)
    for d in range(1, n_col):
        pl.semaphore_signal(barrier, inc=1, device_id={"col": (col + d) % n_col}, device_id_type=MESH)
    for d in range(n_col):
        pl.semaphore_signal(barrier, inc=1, device_id={"col": (col + d) % n_col, "vec": oth}, device_id_type=MESH)
    pltpu.make_async_copy(x_mine, x_mine, mine_sem).wait()
    pl.semaphore_wait(barrier, n_row - 1 + 2 * n_col - 1)

    def remote(src, dst, send, recv, to):
        return pltpu.make_async_remote_copy(
            src_ref=src, dst_ref=dst, send_sem=send, recv_sem=recv, device_id=to, device_id_type=MESH
        )

    far = sorted(range(1, n_z), key=lambda d: -min(d, n_z - d))

    def owned(k):
        return pl.ds(k * ch, ch)

    def x_up(d):
        return remote(x_mine, x_col.at[owned(row)], x_s, xz_r, {"row": (row + 2 * d) % n_row})

    def x_side(d):
        return remote(x_mine, x_row.at[owned(col)], x_s, xr_r, {"col": (col + d) % n_col})

    def x_over():
        return remote(x_mine, x_oth.at[owned(col)], x_s, xp_r, {"vec": oth})

    def x_pass(d):
        part = x_oth.at[owned(col)]
        return remote(part, part, x_s, xo_r, {"col": (col + d) % n_col})

    x_over().start()
    for d in far:
        @pl.when(z + d < n_z)
        def _():
            x_up(d).start()
    for d in range(1, n_col):
        x_side(d).start()
    x_row[owned(col)] = x_mine[...]
    x_col[owned(row)] = x_mine[...]
    for k in range(2, n_row):
        @pl.when(k // 2 > z)
        def _():
            x_col[owned(k)] = jnp.zeros((ch, vloc, tile), BF16)
    for q in lists:
        q.wait()
    rows_l = rows_v[0]
    cols_l = cols_v[0]
    live = lax.broadcasted_iota(jnp.int32, (1, slots), 1) < count_v[0:1, 0:1]

    mate = {"row": row + 1 - 2 * core}

    def x_mate():
        return remote(x_mine, x_col.at[owned(row)], x_s, xf_r, mate)

    def x_forward(zz):
        part = x_col.at[owned(2 * zz + core)]
        return remote(part, part, x_s, xf_r, mate)

    x_mate().start()

    def bytes_of(ref, sem):
        pltpu.make_async_copy(ref, ref, sem).wait()

    def by_z(ref, unit, count, sem):
        for k in range(n_z):
            if count(k):
                @pl.when(z == k)
                def _():
                    bytes_of(ref.at[pl.ds(0, count(k) * unit)], sem)

    bytes_of(tiles, tile_sem)

    def flip(c, carry):
        for q in range(per):
            flipped[c * per + q] = jnp.transpose(tiles[c * per + q])
        return carry

    lax.fori_loop(0, CHUNKS, flip, 0)

    bytes_of(x_oth.at[owned(col)], xp_r)
    for d in range(1, n_col):
        x_pass(d).start()
    bytes_of(x_row.at[pl.ds(0, (n_col - 1) * ch)], xr_r)

    zero = jnp.zeros((vloc, tile), BF16)

    def two(pick, first, out, held):
        left = jnp.concatenate(
            [
                jnp.concatenate([pick(first), zero], 1),
                jnp.concatenate([zero, pick(first + 1)], 1),
            ],
            0,
        )
        w = jnp.concatenate([held[first], held[first + 1]], 0)
        out[first * vloc:(first + 2) * vloc, :] = jnp.dot(left, w, preferred_element_type=F32)

    def pick_row(t):
        return x_row[rows_s[0, 0, t] & (span - 1)]

    def pick_col(t):
        c = cols_s[0, 0, t]
        return x_col[lax.shift_right_logical(c, span_bits) * ch + (c & (ch - 1))]

    for t in range(0, slots, 2):
        two(pick_row, t, upper, tiles)

    by_z(x_col, ch, lambda k: k, xz_r)
    for d in far:
        @pl.when(z - d >= 0)
        def _():
            x_forward(z - d).start()

    for t in range(slots, slots, 2):
        two(pick_row, t, upper, tiles)

    def scatter(src, hot, dst):
        m = hot.shape[0]
        for p in range(vloc // 2):
            both = jnp.concatenate(
                [src[pl.ds(2 * p, slots, stride=vloc), :], src[pl.ds(2 * p + 1, slots, stride=vloc), :]], 1
            )
            hi, lo = split_hi_lo(both)
            res = jnp.dot(hot, hi, preferred_element_type=F32) + jnp.dot(hot, lo, preferred_element_type=F32)
            dst[pl.ds(2 * p, m, stride=vloc), :] = res[:, :tile]
            dst[pl.ds(2 * p + 1, m, stride=vloc), :] = res[:, tile:]

    def one_hot(place, m):
        hit = lax.broadcasted_iota(jnp.int32, (m, slots), 0) == place
        return jnp.where(hit, 1.0, 0.0).astype(BF16)

    group = cols_l // span
    col_place = (group % 2) * (n_z * ch) + (group // 2) * ch + cols_l % ch
    scatter(upper, one_hot(jnp.where(live & (rows_l != cols_l), col_place, -1), n_row * ch), col_part)

    half = n_z * blk

    def z_block(zz):
        return pl.ds(pl.multiple_of(zz * blk, blk), blk)

    def swap(d):
        give = pl.ds(pl.multiple_of((1 - core) * half + (z - d) * blk, blk), blk)
        return remote(col_part.at[give], exch.at[z_block(z - d)], z_s, ex_r, mate)

    near = far + [0]
    for d in near:
        @pl.when(z - d >= 0)
        def _():
            swap(d).start()

    by_z(x_col, ch, lambda k: k + 1, xf_r)

    def z_send(d):
        return remote(
            z_acc.at[z_block(z - d)], z_recv.at[z], z_s, zs_r, {"row": row - 2 * d}
        )

    for t in range(0, slots, 2):
        two(pick_col, t, down, flipped)

    by_z(exch, blk, lambda k: k + 1, ex_r)
    for d in near:
        @pl.when(z - d >= 0)
        def _():
            keep = pl.ds(pl.multiple_of(core * half + (z - d) * blk, blk), blk)
            z_acc[z_block(z - d), :] = col_part[keep, :] + exch[z_block(z - d), :]
            if d:
                z_send(d).start()


    row_hot = jnp.concatenate(
        [
            one_hot(jnp.where(live, rows_l % span, -1), span),
            one_hot(jnp.where(live & (rows_l == cols_l), rows_l % ch, -1), 2 * ch),
        ],
        0,
    )
    scatter(down, row_hot, row_part)

    def r_send(d):
        to = (col + d) % n_col
        return remote(
            row_part.at[pl.ds(pl.multiple_of(to * blk, blk), blk)], row_recv.at[col], o_s, rs_r,
            {"col": to},
        )

    bytes_of(x_oth.at[pl.ds(0, (n_col - 1) * ch)], xo_r)

    def against(base, j):
        part = jnp.concatenate(
            [row_part[pl.ds(base + m * vloc, vloc), :] for m in range(ch)], 1
        )
        hi, lo = split_hi_lo(part)
        left = jnp.concatenate([hi, lo], 0)
        right = jnp.concatenate(
            [
                jnp.concatenate([x[j * ch + m] for m in range(ch)], 1)
                for x in (x_row, x_oth)
            ],
            0,
        )
        r = lax.dot_general(left, right, (((1,), (1,)), ((), ())), preferred_element_type=F32)
        return r[:vloc] + r[vloc:]

    whole = against(0, 0)
    for jj in range(1, n_col):
        whole = whole + against(jj * blk, jj)
    off = whole - against(span * vloc, col)
    pad = jnp.zeros((vloc, tile - 4 * vloc), F32)
    wide = jnp.concatenate([off, whole, pad], 1)
    packed = jnp.concatenate([wide[:1], wide[fold:fold + 1]], 0)
    for k in range(1, fold):
        pair = jnp.concatenate([wide[k:k + 1], wide[fold + k:fold + k + 1]], 0)
        packed = packed + pltpu.roll(pair, 4 * vloc * k, 1)
    g1_send[...] = packed
    g1_recv[vec * n_col + col] = packed

    def g1_side(d):
        return remote(g1_send, g1_recv.at[vec * n_col + col], o_s, g1_r, {"col": (col + d) % n_col})

    def g1_over(d):
        return remote(
            g1_send, g1_recv.at[vec * n_col + col], o_s, g1_r,
            {"col": (col + d) % n_col, "vec": oth},
        )

    for d in range(n_col):
        g1_over(d).start()
    for d in range(1, n_col):
        g1_side(d).start()
    for d in range(1, n_col):
        r_send(d).start()

    bytes_of(g1_recv.at[pl.ds(0, 2 * n_col - 1)], g1_r)
    own = g1_recv[vec * n_col]
    other = g1_recv[oth * n_col]
    for d in range(1, n_col):
        own = own + g1_recv[vec * n_col + d]
        other = other + g1_recv[oth * n_col + d]
    both = jnp.concatenate([own, other], 0)
    g2_send[...] = both
    g2_recv[row] = both

    def g2(d):
        return remote(g2_send, g2_recv.at[row], o_s, g2_r, {"row": (row + d) % n_row})

    order = sorted(range(1, n_row), key=lambda d: -min(d, n_row - d))
    for d in order:
        g2(d).start()

    bytes_of(row_recv.at[pl.ds(0, n_col - 1)], rs_r)
    image = row_part[pl.ds(pl.multiple_of(col * blk, blk), blk), :] + z_acc[z_block(z), :]
    for d in range(1, n_col):
        image = image + row_recv[(col + d) % n_col]
    acc[...] = image
    by_z(z_recv, 1, lambda k: n_z - 1 - k, zs_r)
    for d in range(n_z - 1, 0, -1):
        @pl.when(z + d < n_z)
        def _():
            acc[...] += z_recv[(z + d) % n_z]

    for m in range(ch):
        prod_ref[:, m * tile:(m + 1) * tile] = acc[m * vloc:(m + 1) * vloc, :].astype(BF16)

    bytes_of(g2_recv.at[pl.ds(0, n_row - 1)], g2_r)
    total = g2_recv[0]
    for d in range(1, n_row):
        total = total + g2_recv[d]

    def unpack(q):
        lines = [total[q:q + 2]] + [pltpu.roll(total[q:q + 2], tile - 4 * vloc * k, 1) for k in range(1, fold)]
        return jnp.concatenate([lines[k][p:p + 1] for p in range(2) for k in range(fold)], 0)

    mine = unpack(0)
    theirs = unpack(2)
    g_own = mine[:, 2 * vloc:3 * vloc] + jnp.transpose(mine)[:vloc, :vloc]
    g_oth = mine[:, 3 * vloc:4 * vloc] + jnp.transpose(theirs)[vloc:2 * vloc, :vloc]
    first = jnp.where(vec == 0, g_own, g_oth)
    second = jnp.where(vec == 0, g_oth, g_own)
    gram_ref[...] = jnp.concatenate([first, second], 1) * scale

    x_sends = n_z + 2 * n_col - 1
    bytes_of(upper.at[pl.ds(0, x_sends * blk // 2)], x_s)
    by_z(upper, blk, lambda k: 2 * k + 1, z_s)
    bytes_of(upper.at[pl.ds(0, (n_col - 1) * blk + (2 * n_col - 1) * 2 + (n_row - 1) * 4)], o_s)


def hand_over(prod_ref, gram_ref, prod_out, gram_out, sem):
    one = pltpu.make_async_copy(prod_ref, prod_out, sem.at[0])
    two = pltpu.make_async_copy(gram_ref, gram_out, sem.at[1])
    one.start()
    two.start()
    one.wait()
    two.wait()


def shards(n_row, n_col, vectors, tile_vals, tile_rows, tile_cols, tile_counts):
    vloc, width = vectors.shape
    slots, tile = tile_vals.shape[2], tile_vals.shape[3]
    ch = width // tile
    blk = ch * vloc
    n_z = n_row // 2
    dma = pltpu.SemaphoreType.DMA
    vmem = functools.partial(pl.BlockSpec, memory_space=pltpu.VMEM)
    scale = 1.0 / math.sqrt(width * n_row * n_col)
    counted = pltpu.with_memory_space_constraint(jnp.pad(tile_counts, ((0, 0), (0, tile - 1))), pltpu.VMEM)
    product, gram = pl.pallas_call(
        functools.partial(kernel, n_row, n_col, scale),
        out_shape=(
            pltpu.VMEM((vloc, width), BF16),
            pltpu.VMEM((vloc, 2 * vloc), F32),
        ),
        in_specs=[vmem()] + [pl.BlockSpec(memory_space=pltpu.HBM)] * 4,
        out_specs=(vmem(), vmem()),
        scratch_shapes=[
            pltpu.SMEM((1, 1, slots), jnp.int32),
            pltpu.SMEM((1, 1, slots), jnp.int32),
            pltpu.VMEM((1, 1, slots), jnp.int32),
            pltpu.VMEM((1, 1, slots), jnp.int32),
            pltpu.VMEM((slots, tile, tile), BF16),
            pltpu.VMEM((slots, tile, tile), BF16),
            pltpu.VMEM((ch, vloc, tile), BF16),
            pltpu.VMEM((n_col * ch, vloc, tile), BF16),
            pltpu.VMEM((n_col * ch, vloc, tile), BF16),
            pltpu.VMEM((n_row * ch, vloc, tile), BF16),
            pltpu.VMEM((slots * vloc, tile), F32),
            pltpu.VMEM((slots * vloc, tile), F32),
            pltpu.VMEM((n_row * blk, tile), F32),
            pltpu.VMEM((n_z * blk, tile), F32),
            pltpu.VMEM((n_z * blk, tile), F32),
            pltpu.VMEM((n_z, blk, tile), F32),
            pltpu.VMEM(((n_col + 2) * blk, tile), F32),
            pltpu.VMEM((n_col, blk, tile), F32),
            pltpu.VMEM((blk, tile), F32),
            pltpu.VMEM((2, tile), F32),
            pltpu.VMEM((2 * n_col, 2, tile), F32),
            pltpu.VMEM((4, tile), F32),
            pltpu.VMEM((n_row, 4, tile), F32),
            dma((4,)), *([dma(())] * 15),
        ],
        compiler_params=pltpu.CompilerParams(
            collective_id=0, has_side_effects=True, vmem_limit_bytes=60 * 1024 * 1024
        ),
    )(counted, tile_rows, tile_cols, vectors, tile_vals)
    product, gram = pl.pallas_call(
        hand_over,
        out_shape=(
            jax.ShapeDtypeStruct((vloc, width), BF16),
            jax.ShapeDtypeStruct((vloc, 2 * vloc), F32),
        ),
        in_specs=[vmem(), vmem()],
        out_specs=(pl.BlockSpec(memory_space=pl.ANY), pl.BlockSpec(memory_space=pl.ANY)),
        scratch_shapes=[dma((2,))],
    )(pltpu.with_memory_space_constraint(product, pltpu.VMEM), pltpu.with_memory_space_constraint(gram, pltpu.VMEM))
    return product, gram.T


def solution(mesh):
    return jax.shard_map(
        functools.partial(shards, mesh.shape["row"], mesh.shape["col"]),
        mesh=mesh,
        in_specs=(
            P("vec", ("row", "col")),
            P("row", "col", None, None, None),
            P("row", "col", None),
            P("row", "col", None),
            P("row", "col"),
        ),
        out_specs=(P("vec", ("row", "col")), P(None, "vec")),
        check_vma=False,
    )
```

```python
import functools
import math

import jax
import jax.numpy as jnp
from jax import lax
from jax.experimental import pallas as pl
from jax.experimental.pallas import tpu as pltpu
from jax.sharding import PartitionSpec as P

MESH = pl.DeviceIdType.MESH
BF16 = jnp.bfloat16
F32 = jnp.float32
CHUNKS = 4


def split_hi_lo(value):
    hi = value.astype(BF16)
    lo = (value - hi.astype(F32)).astype(BF16)
    return hi, lo


def kernel(
    n_row, n_col, scale,
    count_v, rows_hbm, cols_hbm, x_ref, tiles_hbm,
    prod_ref, gram_ref,
    rows_s, cols_s, rows_v, cols_v, tiles, flipped, x_mine, x_row, x_oth, x_col, upper, down, col_part, exch, z_acc, z_recv, row_part, row_recv, acc,
    g1_send, g1_recv, g2_send, g2_recv,
    list_sem, mine_sem, tile_sem, x_s, xz_r, xf_r, xr_r, xp_r, xo_r, z_s, ex_r, zs_r, o_s, rs_r, g1_r, g2_r,
):
    n_z = n_row // 2
    slots = tiles.shape[0]
    tile = tiles.shape[1]
    vloc = x_ref.shape[0]
    ch = x_ref.shape[1] // tile
    blk = ch * vloc
    span = n_col * ch
    per = slots // CHUNKS
    fold = vloc // 2
    span_bits = span.bit_length() - 1
    row = lax.axis_index("row")
    col = lax.axis_index("col")
    vec = lax.axis_index("vec")
    z = row // 2
    core = row % 2
    oth = 1 - vec

    def tile_copy(c):
        part = pl.ds(c * per, per)
        return pltpu.make_async_copy(tiles_hbm.at[0, 0, part], tiles.at[part], tile_sem)

    def mine_copy(m):
        return pltpu.make_async_copy(x_ref.at[:, pl.ds(m * tile, tile)], x_mine.at[m], mine_sem)

    lists = [
        pltpu.make_async_copy(rows_hbm, rows_s, list_sem.at[0]),
        pltpu.make_async_copy(cols_hbm, cols_s, list_sem.at[1]),
        pltpu.make_async_copy(cols_hbm, cols_v, list_sem.at[2]),
        pltpu.make_async_copy(rows_hbm, rows_v, list_sem.at[3]),
    ]

    for m in range(ch):
        mine_copy(m).start()
    for q in lists:
        q.start()
    for c in range(CHUNKS):
        tile_copy(c).start()

    barrier = pltpu.get_barrier_semaphore()
    for d in range(1, n_row):
        pl.semaphore_signal(barrier, inc=1, device_id={"row": (row + d) % n_row}, device_id_type=MESH)
    for d in range(1, n_col):
        pl.semaphore_signal(barrier, inc=1, device_id={"col": (col + d) % n_col}, device_id_type=MESH)
    for d in range(n_col):
        pl.semaphore_signal(barrier, inc=1, device_id={"col": (col + d) % n_col, "vec": oth}, device_id_type=MESH)
    pltpu.make_async_copy(x_mine, x_mine, mine_sem).wait()
    pl.semaphore_wait(barrier, n_row - 1 + 2 * n_col - 1)

    def remote(src, dst, send, recv, to):
        return pltpu.make_async_remote_copy(
            src_ref=src, dst_ref=dst, send_sem=send, recv_sem=recv, device_id=to, device_id_type=MESH
        )

    far = sorted(range(1, n_z), key=lambda d: -min(d, n_z - d))

    def owned(k):
        return pl.ds(k * ch, ch)

    def x_up(d):
        return remote(x_mine, x_col.at[owned(row)], x_s, xz_r, {"row": (row + 2 * d) % n_row})

    def x_side(d):
        return remote(x_mine, x_row.at[owned(col)], x_s, xr_r, {"col": (col + d) % n_col})

    def x_over():
        return remote(x_mine, x_oth.at[owned(col)], x_s, xp_r, {"vec": oth})

    def x_pass(d):
        part = x_oth.at[owned(col)]
        return remote(part, part, x_s, xo_r, {"col": (col + d) % n_col})

    x_over().start()
    for d in far:
        @pl.when(z + d < n_z)
        def _():
            x_up(d).start()
    for d in range(1, n_col):
        x_side(d).start()
    x_row[owned(col)] = x_mine[...]
    x_col[owned(row)] = x_mine[...]
    for k in range(2, n_row):
        @pl.when(k // 2 > z)
        def _():
            x_col[owned(k)] = jnp.zeros((ch, vloc, tile), BF16)
    for q in lists:
        q.wait()
    rows_l = rows_v[0]
    cols_l = cols_v[0]
    live = lax.broadcasted_iota(jnp.int32, (1, slots), 1) < count_v[0:1, 0:1]

    mate = {"row": row + 1 - 2 * core}

    def x_mate():
        return remote(x_mine, x_col.at[owned(row)], x_s, xf_r, mate)

    def x_forward(zz):
        part = x_col.at[owned(2 * zz + core)]
        return remote(part, part, x_s, xf_r, mate)

    x_mate().start()

    def bytes_of(ref, sem):
        pltpu.make_async_copy(ref, ref, sem).wait()

    def by_z(ref, unit, count, sem):
        for k in range(n_z):
            if count(k):
                @pl.when(z == k)
                def _():
                    bytes_of(ref.at[pl.ds(0, count(k) * unit)], sem)

    bytes_of(tiles, tile_sem)

    def flip(c, carry):
        for q in range(per):
            flipped[c * per + q] = jnp.transpose(tiles[c * per + q])
        return carry

    lax.fori_loop(0, CHUNKS, flip, 0)

    bytes_of(x_oth.at[owned(col)], xp_r)
    for d in range(1, n_col):
        x_pass(d).start()
    bytes_of(x_row.at[pl.ds(0, (n_col - 1) * ch)], xr_r)

    zero = jnp.zeros((vloc, tile), BF16)

    def two(pick, first, out, held):
        left = jnp.concatenate(
            [
                jnp.concatenate([pick(first), zero], 1),
                jnp.concatenate([zero, pick(first + 1)], 1),
            ],
            0,
        )
        w = jnp.concatenate([held[first], held[first + 1]], 0)
        out[first * vloc:(first + 2) * vloc, :] = jnp.dot(left, w, preferred_element_type=F32)

    def pick_row(t):
        return x_row[rows_s[0, 0, t] & (span - 1)]

    def pick_col(t):
        c = cols_s[0, 0, t]
        return x_col[lax.shift_right_logical(c, span_bits) * ch + (c & (ch - 1))]

    for t in range(0, slots, 2):
        two(pick_row, t, upper, tiles)

    by_z(x_col, ch, lambda k: k, xz_r)
    for d in far:
        @pl.when(z - d >= 0)
        def _():
            x_forward(z - d).start()

    for t in range(slots, slots, 2):
        two(pick_row, t, upper, tiles)

    def scatter(src, hot, dst):
        m = hot.shape[0]
        for p in range(vloc // 2):
            both = jnp.concatenate(
                [src[pl.ds(2 * p, slots, stride=vloc), :], src[pl.ds(2 * p + 1, slots, stride=vloc), :]], 1
            )
            hi, lo = split_hi_lo(both)
            res = jnp.dot(hot, hi, preferred_element_type=F32) + jnp.dot(hot, lo, preferred_element_type=F32)
            dst[pl.ds(2 * p, m, stride=vloc), :] = res[:, :tile]
            dst[pl.ds(2 * p + 1, m, stride=vloc), :] = res[:, tile:]

    def one_hot(place, m):
        hit = lax.broadcasted_iota(jnp.int32, (m, slots), 0) == place
        return jnp.where(hit, 1.0, 0.0).astype(BF16)

    group = cols_l // span
    col_place = (group % 2) * (n_z * ch) + (group // 2) * ch + cols_l % ch
    scatter(upper, one_hot(jnp.where(live & (rows_l != cols_l), col_place, -1), n_row * ch), col_part)

    half = n_z * blk

    def z_block(zz):
        return pl.ds(pl.multiple_of(zz * blk, blk), blk)

    def swap(d):
        give = pl.ds(pl.multiple_of((1 - core) * half + (z - d) * blk, blk), blk)
        return remote(col_part.at[give], exch.at[z_block(z - d)], z_s, ex_r, mate)

    near = far + [0]
    for d in near:
        @pl.when(z - d >= 0)
        def _():
            swap(d).start()

    by_z(x_col, ch, lambda k: k + 1, xf_r)

    def z_send(d):
        return remote(
            z_acc.at[z_block(z - d)], z_recv.at[z], z_s, zs_r, {"row": row - 2 * d}
        )

    for t in range(0, slots, 2):
        two(pick_col, t, down, flipped)

    by_z(exch, blk, lambda k: k + 1, ex_r)
    for d in near:
        @pl.when(z - d >= 0)
        def _():
            keep = pl.ds(pl.multiple_of(core * half + (z - d) * blk, blk), blk)
            z_acc[z_block(z - d), :] = col_part[keep, :] + exch[z_block(z - d), :]
            if d:
                z_send(d).start()


    row_hot = jnp.concatenate(
        [
            one_hot(jnp.where(live, rows_l % span, -1), span),
            one_hot(jnp.where(live & (rows_l == cols_l), rows_l % ch, -1), 2 * ch),
        ],
        0,
    )
    scatter(down, row_hot, row_part)

    def r_send(d):
        to = (col + d) % n_col
        return remote(
            row_part.at[pl.ds(pl.multiple_of(to * blk, blk), blk)], row_recv.at[col], o_s, rs_r,
            {"col": to},
        )

    bytes_of(x_oth.at[pl.ds(0, (n_col - 1) * ch)], xo_r)

    def against(base, j):
        part = jnp.concatenate(
            [row_part[pl.ds(base + m * vloc, vloc), :] for m in range(ch)], 1
        )
        hi, lo = split_hi_lo(part)
        left = jnp.concatenate([hi, lo], 0)
        right = jnp.concatenate(
            [
                jnp.concatenate([x[j * ch + m] for m in range(ch)], 1)
                for x in (x_row, x_oth)
            ],
            0,
        )
        r = lax.dot_general(left, right, (((1,), (1,)), ((), ())), preferred_element_type=F32)
        return r[:vloc] + r[vloc:]

    whole = against(0, 0)
    for jj in range(1, n_col):
        whole = whole + against(jj * blk, jj)
    off = whole - against(span * vloc, col)
    pad = jnp.zeros((vloc, tile - 4 * vloc), F32)
    wide = jnp.concatenate([off, whole, pad], 1)
    packed = jnp.concatenate([wide[:1], wide[fold:fold + 1]], 0)
    for k in range(1, fold):
        pair = jnp.concatenate([wide[k:k + 1], wide[fold + k:fold + k + 1]], 0)
        packed = packed + pltpu.roll(pair, 4 * vloc * k, 1)
    g1_send[...] = packed
    g1_recv[vec * n_col + col] = packed

    def g1_side(d):
        return remote(g1_send, g1_recv.at[vec * n_col + col], o_s, g1_r, {"col": (col + d) % n_col})

    def g1_over(d):
        return remote(
            g1_send, g1_recv.at[vec * n_col + col], o_s, g1_r,
            {"col": (col + d) % n_col, "vec": oth},
        )

    for d in range(n_col):
        g1_over(d).start()
    for d in range(1, n_col):
        g1_side(d).start()
    for d in range(1, n_col):
        r_send(d).start()

    bytes_of(g1_recv.at[pl.ds(0, 2 * n_col - 1)], g1_r)
    own = g1_recv[vec * n_col]
    other = g1_recv[oth * n_col]
    for d in range(1, n_col):
        own = own + g1_recv[vec * n_col + d]
        other = other + g1_recv[oth * n_col + d]
    both = jnp.concatenate([own, other], 0)
    g2_send[...] = both
    g2_recv[row] = both

    def g2(d):
        return remote(g2_send, g2_recv.at[row], o_s, g2_r, {"row": (row + d) % n_row})

    order = sorted(range(1, n_row), key=lambda d: -min(d, n_row - d))
    for d in order:
        g2(d).start()

    bytes_of(row_recv.at[pl.ds(0, n_col - 1)], rs_r)
    image = row_part[pl.ds(pl.multiple_of(col * blk, blk), blk), :] + z_acc[z_block(z), :]
    for d in range(1, n_col):
        image = image + row_recv[(col + d) % n_col]
    acc[...] = image
    by_z(z_recv, 1, lambda k: n_z - 1 - k, zs_r)
    for d in range(n_z - 1, 0, -1):
        @pl.when(z + d < n_z)
        def _():
            acc[...] += z_recv[(z + d) % n_z]

    for m in range(ch):
        prod_ref[:, m * tile:(m + 1) * tile] = acc[m * vloc:(m + 1) * vloc, :].astype(BF16)

    bytes_of(g2_recv.at[pl.ds(0, n_row - 1)], g2_r)
    total = g2_recv[0]
    for d in range(1, n_row):
        total = total + g2_recv[d]

    def unpack(q):
        lines = [total[q:q + 2]] + [pltpu.roll(total[q:q + 2], tile - 4 * vloc * k, 1) for k in range(1, fold)]
        return jnp.concatenate([lines[k][p:p + 1] for p in range(2) for k in range(fold)], 0)

    mine = unpack(0)
    theirs = unpack(2)
    g_own = mine[:, 2 * vloc:3 * vloc] + jnp.transpose(mine)[:vloc, :vloc]
    g_oth = mine[:, 3 * vloc:4 * vloc] + jnp.transpose(theirs)[vloc:2 * vloc, :vloc]
    first = jnp.where(vec == 0, g_own, g_oth)
    second = jnp.where(vec == 0, g_oth, g_own)
    gram_ref[...] = jnp.concatenate([first, second], 1) * scale

    x_sends = n_z + 2 * n_col - 1
    bytes_of(upper.at[pl.ds(0, x_sends * blk // 2)], x_s)
    by_z(upper, blk, lambda k: 2 * k + 1, z_s)
    bytes_of(upper.at[pl.ds(0, (n_col - 1) * blk + (2 * n_col - 1) * 2 + (n_row - 1) * 4)], o_s)


def hand_over(prod_ref, gram_ref, prod_out, gram_out, sem):
    one = pltpu.make_async_copy(prod_ref, prod_out, sem.at[0])
    two = pltpu.make_async_copy(gram_ref, gram_out, sem.at[1])
    one.start()
    two.start()
    one.wait()
    two.wait()


def shards(n_row, n_col, vectors, tile_vals, tile_rows, tile_cols, tile_counts):
    vloc, width = vectors.shape
    slots, tile = tile_vals.shape[2], tile_vals.shape[3]
    ch = width // tile
    blk = ch * vloc
    n_z = n_row // 2
    dma = pltpu.SemaphoreType.DMA
    vmem = functools.partial(pl.BlockSpec, memory_space=pltpu.VMEM)
    scale = 1.0 / math.sqrt(width * n_row * n_col)
    counted = pltpu.with_memory_space_constraint(jnp.pad(tile_counts, ((0, 0), (0, tile - 1))), pltpu.VMEM)
    product, gram = pl.pallas_call(
        functools.partial(kernel, n_row, n_col, scale),
        out_shape=(
            pltpu.VMEM((vloc, width), BF16),
            pltpu.VMEM((vloc, 2 * vloc), F32),
        ),
        in_specs=[vmem()] + [pl.BlockSpec(memory_space=pltpu.HBM)] * 4,
        out_specs=(vmem(), vmem()),
        scratch_shapes=[
            pltpu.SMEM((1, 1, slots), jnp.int32),
            pltpu.SMEM((1, 1, slots), jnp.int32),
            pltpu.VMEM((1, 1, slots), jnp.int32),
            pltpu.VMEM((1, 1, slots), jnp.int32),
            pltpu.VMEM((slots, tile, tile), BF16),
            pltpu.VMEM((slots, tile, tile), BF16),
            pltpu.VMEM((ch, vloc, tile), BF16),
            pltpu.VMEM((n_col * ch, vloc, tile), BF16),
            pltpu.VMEM((n_col * ch, vloc, tile), BF16),
            pltpu.VMEM((n_row * ch, vloc, tile), BF16),
            pltpu.VMEM((slots * vloc, tile), F32),
            pltpu.VMEM((slots * vloc, tile), F32),
            pltpu.VMEM((n_row * blk, tile), F32),
            pltpu.VMEM((n_z * blk, tile), F32),
            pltpu.VMEM((n_z * blk, tile), F32),
            pltpu.VMEM((n_z, blk, tile), F32),
            pltpu.VMEM(((n_col + 2) * blk, tile), F32),
            pltpu.VMEM((n_col, blk, tile), F32),
            pltpu.VMEM((blk, tile), F32),
            pltpu.VMEM((2, tile), F32),
            pltpu.VMEM((2 * n_col, 2, tile), F32),
            pltpu.VMEM((4, tile), F32),
            pltpu.VMEM((n_row, 4, tile), F32),
            dma((4,)), *([dma(())] * 15),
        ],
        compiler_params=pltpu.CompilerParams(
            collective_id=0, has_side_effects=True, vmem_limit_bytes=60 * 1024 * 1024
        ),
    )(counted, tile_rows, tile_cols, vectors, tile_vals)
    product, gram = pl.pallas_call(
        hand_over,
        out_shape=(
            jax.ShapeDtypeStruct((vloc, width), BF16),
            jax.ShapeDtypeStruct((vloc, 2 * vloc), F32),
        ),
        in_specs=[vmem(), vmem()],
        out_specs=(pl.BlockSpec(memory_space=pl.ANY), pl.BlockSpec(memory_space=pl.ANY)),
        scratch_shapes=[dma((2,))],
    )(pltpu.with_memory_space_constraint(product, pltpu.VMEM), pltpu.with_memory_space_constraint(gram, pltpu.VMEM))
    return product, gram.T


def solution(mesh):
    return jax.shard_map(
        functools.partial(shards, mesh.shape["row"], mesh.shape["col"]),
        mesh=mesh,
        in_specs=(
            P("vec", ("row", "col")),
            P("row", "col", None, None, None),
            P("row", "col", None),
            P("row", "col", None),
            P("row", "col"),
        ),
        out_specs=(P("vec", ("row", "col")), P(None, "vec")),
        check_vma=False,
    )
```
